32 devices in a mesh: trow: 4 (over y, x), tcol: 4 (over z), pix: 2 (over core).
Axes of the slice: x: 2, y: 2, z: 4, core: 2. Of those that a mesh axis runs over, the one named last changes fastest.
Arguments:
- frames: float32 [6144, 2, 64, 128], P(('trow', 'tcol'), None, 'pix'), may hold values from 0.1 to 8
- drift: int32 [6144, 2], P(('trow', 'tcol')), may hold values from -7 to 7
Outputs:
- inner_cycle: float32 [6144, 6144], P(('trow', 'pix'), 'tcol')
- second_band_twotime: float32 [6144, 6144], P(('trow', 'pix'), 'tcol')
The draws below stay inside these ranges and needn't reach their ends.
All inputs are finite; a program needn't handle non-finite values.
Results may differ from the reference program's by a relative error of at most 0.0003.
Values may be sent and summed in bfloat16 or wider, within the bound.
No kernel may reach another device: no remote copies, remote signals or barrier semaphores. Data moves between devices by JAX's collectives and lax.ppermute only.
A program may use at most 192 MiB of HBM per device.

```python
import math
import jax
import jax.numpy as jnp
from jax import lax

RB = 64
COLS = 128
EXPOSURE_TALLY = 6144
PB = 8192


def draw_frames(key, part):
    pixel_shape = (2, RB, COLS)
    key_pixel = jax.random.fold_in(key, 101)
    key_frame = jax.random.fold_in(key, 102)
    key_phase = jax.random.fold_in(key, 103)
    flurry_seed_handle = jax.random.fold_in(key, 104)
    key_static = jax.random.fold_in(key, 105)
    key_start = jax.random.fold_in(key, 106)
    key_noise = jax.random.fold_in(key, 107)
    pixel_low, pixel_high = (0.3, 3.0)
    pixel_level = jnp.exp(jax.random.uniform(key_pixel, pixel_shape, jnp.float32, math.log(pixel_low), math.log(pixel_high)))
    frame_level = jnp.exp(jax.random.uniform(key_frame, (EXPOSURE_TALLY,), jnp.float32, math.log(0.3), math.log(3.0)))
    progress = jnp.arange(EXPOSURE_TALLY, dtype=jnp.float32) / EXPOSURE_TALLY
    grain_decay_period = 40.0 * 12.5 ** progress
    phase_offset = jax.random.uniform(key_phase, (), jnp.float32, 0.0, 1.0)
    share = 0.35 + 0.3 * jnp.sin(2.0 * math.pi * (1.5 * progress + phase_offset))
    exposure_flurry_stack = jax.random.randint(flurry_seed_handle, (6,), 0, EXPOSURE_TALLY)
    flurry_enabled = jnp.any(jnp.arange(EXPOSURE_TALLY, dtype=jnp.int32)[:, None] == exposure_flurry_stack[None, :], axis=1)
    recall_store = jnp.where(flurry_enabled, 0.3, jnp.exp(-1.0 / grain_decay_period)).astype(jnp.float32)
    static_field = jax.random.normal(key_static, (2,) + pixel_shape, jnp.float32) * math.sqrt(0.5)
    start_field = jax.random.normal(key_start, (2,) + pixel_shape, jnp.float32) * math.sqrt(0.5)

    def advance(carried_state, inputs):
        frame_index, decay_rate, fraction, frame_gain = inputs
        fresh = jax.random.normal(jax.random.fold_in(key_noise, frame_index), (2,) + pixel_shape, jnp.float32) * math.sqrt(0.5)
        carried_state = decay_rate * carried_state + jnp.sqrt(1.0 - decay_rate * decay_rate) * fresh
        amplitude = jnp.sqrt(1.0 - fraction) * carried_state + jnp.sqrt(fraction) * static_field
        intensity = amplitude[0] * amplitude[0] + amplitude[1] * amplitude[1]
        return (carried_state, jnp.minimum(0.1 + 0.5 * frame_gain * pixel_level * intensity, 8.0))
    ignored, series = lax.scan(advance, start_field, (jnp.arange(EXPOSURE_TALLY, dtype=jnp.int32), recall_store, share.astype(jnp.float32), frame_level))
    return series


def plant(values, stream_key, smallest, largest):
    dims = values.shape
    spot = [jax.random.randint(jax.random.fold_in(stream_key, axis), (), 0, dims[axis]) for axis in range(len(dims))]
    values = values.at[tuple(spot)].set(smallest)
    longest = dims.index(max(dims))
    spot[longest] = (spot[longest] + 1) % dims[longest]
    return values.at[tuple(spot)].set(largest)


def setup_inputs(seed: int = 0) -> dict:
    seeds = jax.random.split(jax.random.key(seed), 3)
    frames = draw_frames(jax.random.fold_in(seeds[2], 71), 0)
    drift = plant(jax.random.randint(seeds[1], (EXPOSURE_TALLY, 2), -7, 8), jax.random.fold_in(seeds[1], 1), -7, 7).astype(jnp.int32)
    return dict(frames=frames, drift=drift)


def blend(padded, steps, device_axis):
    upward = (jnp.maximum(steps, 0).astype(jnp.float32) / 8.0)[:, None, None, None]
    downward = (jnp.maximum(-steps, 0).astype(jnp.float32) / 8.0)[:, None, None, None]
    length = padded.shape[device_axis] - 2
    middle = lax.slice_in_dim(padded, 1, 1 + length, 1, device_axis)
    after = lax.slice_in_dim(padded, 2, 2 + length, 1, device_axis)
    before = lax.slice_in_dim(padded, 0, length, 1, device_axis)
    return (1.0 - upward - downward) * middle + upward * after + downward * before


def reference(frames, drift):
    padded = jnp.pad(frames, ((0, 0), (0, 0), (1, 1), (0, 0)))
    rowpass = blend(padded, drift[:, 0], 2)
    padded = jnp.pad(rowpass, ((0, 0), (0, 0), (0, 0), (1, 1)))
    shifted = blend(padded, drift[:, 1], 3)
    pixel_mean = jnp.sum(shifted, axis=0) / EXPOSURE_TALLY
    flat = shifted / pixel_mean[None]
    frame_mean = jnp.sum(flat, axis=(2, 3)) / PB
    normed = (flat / frame_mean[:, :, None, None]).astype(jnp.bfloat16)
    results = []
    for band in range(2):
        band_data = normed[:, band].reshape(EXPOSURE_TALLY, PB).astype(jnp.float32)
        gram_full = jnp.dot(band_data, band_data.T, precision=lax.Precision.HIGHEST, preferred_element_type=jnp.float32)
        results.append(gram_full / PB)
    return results[0], results[1]
```

```python
import jax
import jax.numpy as jnp
from jax import lax
from jax.sharding import PartitionSpec as P

PIECES = 2
SHIP = jnp.float16


def extended(cells, axis, dim):
    count = lax.axis_size(axis)
    ends = count - 1
    head = lax.slice_in_dim(cells, 0, 1, axis=dim).astype(jnp.bfloat16)
    size = cells.shape[dim]
    tail = lax.slice_in_dim(cells, size - 1, size, axis=dim).astype(jnp.bfloat16)
    return jnp.concatenate(
        [
            lax.ppermute(tail, axis, [(i, i + 1) for i in range(ends)]).astype(cells.dtype),
            cells,
            lax.ppermute(head, axis, [(i + 1, i) for i in range(ends)]).astype(cells.dtype),
        ],
        axis=dim,
    )


def blend(padded, steps, device_axis):
    upward = (jnp.maximum(steps, 0).astype(jnp.float32) / 8.0)[:, None, None, None]
    downward = (jnp.maximum(-steps, 0).astype(jnp.float32) / 8.0)[:, None, None, None]
    length = padded.shape[device_axis] - 2
    middle = lax.slice_in_dim(padded, 1, 1 + length, 1, device_axis)
    after = lax.slice_in_dim(padded, 2, 2 + length, 1, device_axis)
    before = lax.slice_in_dim(padded, 0, length, 1, device_axis)
    return (1.0 - upward - downward) * middle + upward * after + downward * before


def summed(x, axes):
    for axis in axes:
        count = lax.axis_size(axis)
        step = 1
        while step < count:
            x = x + lax.ppermute(x, axis, [(i, i ^ step) for i in range(count)])
            step *= 2
    return x


def per_device(frames, drift):
    local_frames = frames.shape[0]
    tile_rows = frames.shape[2]
    columns = frames.shape[3]
    nt, nc, npix = (lax.axis_size(a) for a in ("trow", "tcol", "pix"))
    assert nt == 4 and nc == 4
    total_frames = local_frames * nt * nc
    pixels = tile_rows * columns
    band_pixels = pixels * npix
    t, z, pix = (lax.axis_index(a) for a in ("trow", "tcol", "pix"))
    grid = ("trow", "tcol")

    padded = extended(frames, "pix", 2)
    rowpass = blend(padded, drift[:, 0], 2)
    padded = jnp.pad(rowpass, ((0, 0), (0, 0), (0, 0), (1, 1)))
    shifted = blend(padded, drift[:, 1], 3)
    pixel_mean = summed(jnp.sum(shifted, axis=0), grid) / total_frames
    flat = shifted / pixel_mean[None]
    frame_mean = summed(jnp.sum(flat, axis=(2, 3)), ("pix",)) / band_pixels
    normed = (flat / frame_mean[:, :, None, None]).astype(jnp.bfloat16)
    normed = normed.reshape(local_frames, 2, pixels).transpose(1, 0, 2)

    upper = z >= 2
    at_end = (z == 0) | (z == nc - 1)
    height = local_frames // PIECES

    def pieces(x):
        return [x[i * height : (i + 1) * height] for i in range(PIECES)]

    band0, band1 = pieces(normed[0]), pieces(normed[1])
    down = [(i + 1, i) for i in range(nc - 1)]
    upward = [(i, i + 1) for i in range(nc - 1)]
    outward = [(1, 0), (2, 3)]
    own, first, second, third = [], [], [], []
    down1, up1, down2, up2 = [], [], [], []
    for i in range(PIECES):
        down1.append(lax.ppermute(band0[i], "tcol", down))
        up1.append(lax.ppermute(band1[i], "tcol", upward))
    for i in range(PIECES):
        own.append(jnp.where(upper, band1[i], band0[i]))
        first.append(jnp.where(upper, up1[i], down1[i]))
        down2.append(lax.ppermute(jnp.where(z == nc - 1, band1[i], down1[i]), "tcol", down))
        up2.append(lax.ppermute(jnp.where(z == 0, band0[i], up1[i]), "tcol", upward))
    for i in range(PIECES):
        second.append(jnp.where(upper, up2[i], down2[i]))
        moved = lax.ppermute(second[i], "tcol", outward)
        third.append(jnp.where(at_end, moved, jnp.where(upper, down2[i], up2[i])))
    stream = own + first + second + third
    blocks = jnp.array([[0, 1, 2, 3], [1, 2, 3, 0], [2, 1, 0, 3], [3, 2, 1, 0]], jnp.int32)
    place = blocks[z]

    index = lambda a, b: a * nc + b
    across = [
        (index(a, b), index(a ^ 1, b)) for a in range(nt) for b in range(nc) if (a & 1) == (b & 1)
    ]
    swap = [(index(a, b), index(a ^ 2, b)) for a in range(nt) for b in range(nc)]
    source = (t & 1) == (z & 1)
    near, far = [], []
    for piece in stream:
        got = lax.ppermute(piece, grid, across)
        near.append(jnp.where(source, piece, got))
        far.append(lax.ppermute(near[-1], grid, swap))

    half = nc // 2
    rows = jnp.zeros((nc * local_frames, pixels), jnp.bfloat16)
    for k in range(nc):
        slot = place[k]
        if npix == 2:
            slot = (((slot // half) ^ pix) * half) + slot % half
        for i in range(PIECES):
            rows = lax.dynamic_update_slice(
                rows, stream[k * PIECES + i], (slot * local_frames + i * height, 0)
            )

    def gram(cols):
        part = lax.dot_general(
            rows, cols, (((1,), (1,)), ((), ())), preferred_element_type=jnp.float32
        )
        if npix == 2:
            cut = part.shape[0] // 2
            total = part[:cut] + lax.ppermute(part[cut:], "pix", [(0, 1), (1, 0)])
        else:
            total = lax.psum_scatter(part, "pix", scatter_dimension=0, tiled=True)
        return total / band_pixels

    same = (t & 2) == (z & 2)
    over = [(i, i ^ 2) for i in range(nc)]
    keep, ship = [], []
    for k in range(nc):
        a = gram(jnp.concatenate(near[k * PIECES : (k + 1) * PIECES]))
        b = gram(jnp.concatenate(far[k * PIECES : (k + 1) * PIECES]))
        keep.append(jnp.where(same, a, b))
        ship.append(lax.ppermute(jnp.where(same, b, a).astype(SHIP), "tcol", over))

    out_rows = nc * local_frames // npix
    outs = [jnp.zeros((out_rows, nc * local_frames), jnp.float32) for _ in range(2)]
    other = blocks[z ^ 2]
    for k in range(nc):
        for band in range(2):
            hit = upper == (band == 1)
            value = jnp.where(hit, keep[k], ship[k].astype(jnp.float32))
            slot = jnp.where(hit, place[k], other[k])
            outs[band] = lax.dynamic_update_slice(outs[band], value, (0, slot * local_frames))
    return outs[0], outs[1]


def solution(mesh):
    in_specs = (P(("trow", "tcol"), None, "pix", None), P(("trow", "tcol"), None))
    out_specs = (P(("trow", "pix"), "tcol"), P(("trow", "pix"), "tcol"))
    return jax.shard_map(
        per_device, mesh=mesh, in_specs=in_specs, out_specs=out_specs, check_vma=False
    )
```

```python
import functools

import jax
import jax.numpy as jnp
from jax import lax
from jax.experimental import pallas as pl
from jax.experimental.pallas import tpu as pltpu
from jax.sharding import PartitionSpec as P


PIECES = 2
SHIP = jnp.float16
EXTRA = 16
GRID = ("trow", "tcol")


def edge_kernel(first_ref, last_ref, head_ref, tail_ref):
    f, rows, cols = first_ref.shape[0], first_ref.shape[2], first_ref.shape[3]
    for ref, out, r in ((first_ref, head_ref, 0), (last_ref, tail_ref, rows - 1)):
        flat = ref.reshape(f * rows, cols)
        out[0] = flat[pl.ds(r, f, stride=rows), :].astype(jnp.bfloat16)


def edges(frames):
    n, bands, rows, cols = frames.shape
    group = min(8, rows)
    fb = n // 2
    block = (fb, 1, group, cols)
    out = pl.BlockSpec((1, fb, cols), lambda b, i: (b, i, 0))
    shape = jax.ShapeDtypeStruct((bands, n, cols), jnp.bfloat16)
    return pl.pallas_call(
        edge_kernel,
        grid=(bands, n // fb),
        in_specs=[
            pl.BlockSpec(block, lambda b, i: (i, b, 0, 0)),
            pl.BlockSpec(block, lambda b, i: (i, b, rows // group - 1, 0)),
        ],
        out_specs=[out, out],
        out_shape=[shape, shape],
        name="edges",
    )(frames, frames)


def shift_kernel(beta_ref, x_ref, lo_ref, hi_ref, d_ref, s0_ref, s1_ref, own_ref, sum_ref, cs):
    f, bands, rows, cols = x_ref.shape
    flat = x_ref.reshape(f * bands * rows, cols)
    steps = d_ref[...]

    def share(v):
        return jnp.broadcast_to(v.astype(jnp.float32) * 0.125, (f, cols))

    lane = lax.broadcasted_iota(jnp.int32, (f, cols), 1)
    by_row, by_col = steps[:, 0:1], steps[:, 1:2]
    up, down = share(jnp.maximum(by_row, 0)), share(jnp.maximum(-by_row, 0))
    cs[0], cs[1], cs[2] = 1.0 - up - down, up, down
    up, down = share(jnp.maximum(by_col, 0)), share(jnp.maximum(-by_col, 0))
    cs[3] = 1.0 - up - down
    cs[4] = jnp.where(lane == cols - 1, 0.0, up)
    cs[5] = jnp.where(lane == 0, 0.0, down)

    @pl.when(pl.program_id(0) == 0)
    def _():
        sum_ref[...] = jnp.zeros_like(sum_ref)

    for band, s_ref in ((0, s0_ref), (1, s1_ref)):

        def row(r):
            if r < 0:
                return lo_ref[band].astype(jnp.float32)
            if r >= rows:
                return hi_ref[band].astype(jnp.float32)
            return flat[pl.ds(band * rows + r, f, stride=bands * rows), :]

        before, here = row(-1), row(0)
        for r in range(rows):
            after = row(r + 1)
            p = cs[0] * here + cs[1] * after + cs[2] * before
            s = cs[3] * p + cs[4] * pltpu.roll(p, cols - 1, 1) + cs[5] * pltpu.roll(p, 1, 1)
            s = s.astype(jnp.bfloat16)
            s_ref[:, r * cols : (r + 1) * cols] = s
            part = jnp.sum(s.astype(jnp.float32).reshape(f // 8, 8, cols), axis=0)
            sum_ref[band, r * 8 : r * 8 + 8, :] += part
            before, here = here, after

        @pl.when(beta_ref[0] == band)
        def _():
            own_ref[...] = s_ref[...]


def shift(beta, frames, lo, hi, drift, start, count):
    _, bands, rows, cols = frames.shape
    fb = count
    while fb > 64 and fb % 2 == 0:
        fb //= 2
    first = start // fb
    edge = pl.BlockSpec((bands, fb, cols), lambda i, _: (0, i + first, 0))
    out = pl.BlockSpec((fb, rows * cols), lambda i, _: (i, 0))
    shape = jax.ShapeDtypeStruct((count, rows * cols), jnp.bfloat16)
    return pl.pallas_call(
        shift_kernel,
        grid_spec=pltpu.PrefetchScalarGridSpec(
            num_scalar_prefetch=1,
            grid=(count // fb,),
            in_specs=[
                pl.BlockSpec((fb, bands, rows, cols), lambda i, _: (i + first, 0, 0, 0)),
                edge,
                edge,
                pl.BlockSpec((fb, 2), lambda i, _: (i + first, 0)),
            ],
            out_specs=[
                out,
                out,
                out,
                pl.BlockSpec((bands, rows * 8, cols), lambda i, _: (0, 0, 0)),
            ],
            scratch_shapes=[pltpu.VMEM((6, fb, cols), jnp.float32)],
        ),
        out_shape=[shape, shape, shape, jax.ShapeDtypeStruct((bands, rows * 8, cols), jnp.float32)],
        cost_estimate=pl.CostEstimate(
            flops=count * bands * rows * cols * 12,
            bytes_accessed=count * bands * rows * cols * 7,
            transcendentals=0,
        ),
        name="shift",
    )(beta, frames, lo, hi, drift)


def gram_kernel(extra, pieces, *refs):
    refs = list(refs)
    e_ref = refs.pop(0) if extra else None
    a_ref = refs.pop(0)
    c_refs, refs = refs[:pieces], refs[pieces:]
    x_ref = refs.pop(0) if extra else None
    o_ref, c_ref = refs
    h = c_refs[0].shape[0]
    dims = (((1,), (1,)), ((), ()))
    dot = functools.partial(lax.dot_general, dimension_numbers=dims, preferred_element_type=jnp.float32)
    first = pl.program_id(0) == 0

    @pl.when(first)
    def _():
        for i, ref in enumerate(c_refs):
            c_ref[i * h : (i + 1) * h, :] = ref[...]

    if not extra:
        o_ref[...] = dot(a_ref[...], c_ref[...])
        return

    @pl.when(first)
    def _():
        both = dot(jnp.concatenate([e_ref[...], a_ref[...]], axis=0), c_ref[...])
        x_ref[...] = both[:EXTRA]
        o_ref[...] = both[EXTRA:]

    @pl.when(jnp.logical_not(first))
    def _():
        o_ref[...] = dot(a_ref[...], c_ref[...])


def gram(rows, start, count, pieces, extra=None):
    depth = rows.shape[1]
    h = pieces[0].shape[0]
    width = h * len(pieces)
    tile = 256
    while count % tile or start % tile:
        tile //= 2
    first = start // tile
    fixed = lambda shape: pl.BlockSpec(shape, lambda i: (0, 0), pipeline_mode=pl.Buffered(1))
    in_specs = [pl.BlockSpec((tile, depth), lambda i: (i + first, 0))]
    in_specs += [fixed((h, depth)) for _ in pieces]
    out_specs = [pl.BlockSpec((tile, width), lambda i: (i, 0))]
    out_shape = [jax.ShapeDtypeStruct((count, width), jnp.float32)]
    args = [rows, *pieces]
    if extra is not None:
        in_specs.insert(0, fixed((EXTRA, depth)))
        out_specs.insert(0, pl.BlockSpec((EXTRA, width), lambda i: (0, 0)))
        out_shape.insert(0, jax.ShapeDtypeStruct((EXTRA, width), jnp.float32))
        args.insert(0, extra)
    return pl.pallas_call(
        functools.partial(gram_kernel, extra is not None, len(pieces)),
        grid=(count // tile,),
        in_specs=in_specs,
        out_specs=out_specs,
        out_shape=out_shape,
        scratch_shapes=[pltpu.VMEM((width, depth), jnp.bfloat16)],
        cost_estimate=pl.CostEstimate(
            flops=2 * count * width * depth,
            bytes_accessed=2 * depth * (count + width) + 4 * count * width,
            transcendentals=0,
        ),
        name="gram",
    )(*args)


def split(x):
    parts = []
    for _ in range(3):
        part = lax.reduce_precision(x, 8, 7)
        parts.append(part.astype(jnp.bfloat16))
        x = x - part
    pad = jnp.zeros((EXTRA - 3,) + x.shape, jnp.bfloat16)
    return jnp.concatenate([jnp.stack(parts), pad])


def per_device(frames, drift):
    local_frames, _, tile_rows, columns = frames.shape
    nt, nc, npix = (lax.axis_size(a) for a in ("trow", "tcol", "pix"))
    assert nt == 4 and nc == 4
    total_frames = local_frames * nt * nc
    pixels = tile_rows * columns
    band_pixels = pixels * npix
    t, z, pix = (lax.axis_index(a) for a in ("trow", "tcol", "pix"))
    upper = z >= 2
    at_end = (z == 0) | (z == nc - 1)
    beta = upper.astype(jnp.int32)
    height = local_frames // PIECES

    head, tail = edges(frames)
    lo = lax.ppermute(tail, "pix", [(i, i + 1) for i in range(npix - 1)])
    hi = lax.ppermute(head, "pix", [(i + 1, i) for i in range(npix - 1)])
    parts = [shift(beta[None], frames, lo, hi, drift, i * height, height) for i in range(PIECES)]
    band0, band1, own, sums = ([part[j] for part in parts] for j in range(4))

    total = sum(sums).reshape(2, tile_rows, 8, columns).sum(axis=2)
    for axis, step in (("trow", 1), ("trow", 2), ("tcol", 1), ("tcol", 2)):
        total = total + lax.ppermute(total, axis, [(i, i ^ step) for i in range(4)])
    mean = (jnp.where(upper, total[1], total[0]) / total_frames).reshape(pixels)
    weight = 1.0 / (mean * mean)

    down = [(i + 1, i) for i in range(nc - 1)]
    upward = [(i, i + 1) for i in range(nc - 1)]
    outward = [(1, 0), (2, 3)]
    down1 = [lax.ppermute(band0[i], "tcol", down) for i in range(PIECES)]
    up1 = [lax.ppermute(band1[i], "tcol", upward) for i in range(PIECES)]
    first, second, third, down2, up2 = [], [], [], [], []
    for i in range(PIECES):
        first.append(jnp.where(upper, up1[i], down1[i]))
        payload = jnp.where(z == nc - 1, band1[i], down1[i])
        down2.append(lax.ppermute(payload, "tcol", down))
        payload = jnp.where(z == 0, band0[i], up1[i])
        up2.append(lax.ppermute(payload, "tcol", upward))
    for i in range(PIECES):
        second.append(jnp.where(upper, up2[i], down2[i]))
        moved = lax.ppermute(second[i], "tcol", outward)
        third.append(jnp.where(at_end, moved, jnp.where(upper, down2[i], up2[i])))
    stream = own + first + second + third
    blocks = [[0, 1, 2, 3], [1, 2, 3, 0], [2, 1, 0, 3], [3, 2, 1, 0]]
    half = nc // 2
    table = []
    for zz in range(nc):
        for pp in range(npix):
            slots = list(blocks[zz])
            if npix == 2:
                slots = [((b // half) ^ pp) * half + b % half for b in slots]
            line = [b * local_frames + i * height for b in slots for i in range(PIECES)]
            for band in range(2):
                line += [b * local_frames for b in blocks[zz if band == zz // half else zz ^ half]]
            table.append(line)
    width = len(table[0])
    line = lax.dynamic_slice(jnp.array(table, jnp.int32), (z * npix + pix, 0), (1, width))
    offsets = [line[0, j] for j in range(width)]

    index = lambda a, b: a * nc + b
    across = [
        (index(a, b), index(a ^ 1, b)) for a in range(nt) for b in range(nc) if (a & 1) == (b & 1)
    ]
    swap = [(index(a, b), index(a ^ 2, b)) for a in range(nt) for b in range(nc)]
    source = (t & 1) == (z & 1)
    near, far = [], []
    for piece in stream:
        got = lax.ppermute(piece, GRID, across)
        near.append(jnp.where(source, piece, got))
        far.append(lax.ppermute(near[-1], GRID, swap))

    rows = jnp.zeros((nc * local_frames, pixels), jnp.bfloat16)
    for k, piece in enumerate(stream):
        scale, piece, _ = lax.optimization_barrier((weight, piece, far[1]))
        value = (piece.astype(jnp.float32) * scale[None]).astype(jnp.bfloat16)
        rows = lax.dynamic_update_slice(rows, value, (offsets[k], 0))
    dims = (((1,), (1,)), ((), ()))
    level = lax.dot_general(rows, split(mean), dims, preferred_element_type=jnp.float32).sum(axis=1)
    count = nc * local_frames // npix
    if npix == 2:
        level = level[:count] + lax.ppermute(level[count:], "pix", [(0, 1), (1, 0)])
    else:
        level = lax.psum_scatter(level, "pix", scatter_dimension=0, tiled=True)
    row_scale = band_pixels / level
    extra = split(1.0 / mean)

    def correlate(cols, gate):
        if npix == 2:
            sums, theirs = gram(rows, count, count, cols, extra)
            theirs = lax.ppermute(theirs, "pix", [(0, 1), (1, 0)])
            sums = sums[:3].sum(axis=0)
            sums = sums + lax.ppermute(sums, "pix", [(0, 1), (1, 0)])
            (total,) = gram(rows, 0, count, cols)
        else:
            sums, part = gram(rows, 0, nc * local_frames, cols, extra)
            sums = lax.psum(sums[:3].sum(axis=0), "pix")
            total = lax.psum_scatter(part, "pix", scatter_dimension=0, tiled=True)
            theirs = jnp.zeros_like(total)
        theirs, gate = lax.optimization_barrier((theirs, gate))
        return (total + theirs) * row_scale[:, None] * (1.0 / sums)[None, :]

    same = (t & 2) == (z & 2)
    over = [(i, i ^ 2) for i in range(nc)]
    outs = [jnp.zeros((count, nc * local_frames), jnp.float32) for _ in range(2)]
    chunks = [(k, 0, PIECES) for k in range(nc - 1)] + [(nc - 1, i, 1) for i in range(PIECES)]
    gate = row_scale
    for k, i, size in chunks:
        lo = k * PIECES + i
        value = correlate(near[lo : lo + size] + far[lo : lo + size], gate)
        a, b = value[:, : size * height], value[:, size * height :]
        keep = jnp.where(same, a, b)
        gate = (jnp.where(same, b, a) - 1.0).astype(SHIP)
        ship = lax.ppermute(gate, "tcol", over).astype(jnp.float32) + 1.0
        for band in range(2):
            at = offsets[nc * PIECES + band * nc + k] + i * height
            outs[band] = lax.dynamic_update_slice(
                outs[band], jnp.where(upper == (band == 1), keep, ship), (0, at)
            )
    return outs[0], outs[1]


def solution(mesh):
    in_specs = (P(("trow", "tcol"), None, "pix", None), P(("trow", "tcol"), None))
    out_specs = (P(("trow", "pix"), "tcol"), P(("trow", "pix"), "tcol"))

    return jax.shard_map(
        per_device, mesh=mesh, in_specs=in_specs, out_specs=out_specs, check_vma=False
    )
```

```python
import functools

import jax
import jax.numpy as jnp
from jax import lax
from jax.experimental import pallas as pl
from jax.experimental.pallas import tpu as pltpu
from jax.sharding import PartitionSpec as P


PIECES = 2
SHIP = jnp.float16
EXTRA = 16
GRID = ("trow", "tcol")


def edge_kernel(first_ref, last_ref, head_ref, tail_ref):
    f, rows, cols = first_ref.shape[0], first_ref.shape[2], first_ref.shape[3]
    for ref, out, r in ((first_ref, head_ref, 0), (last_ref, tail_ref, rows - 1)):
        flat = ref.reshape(f * rows, cols)
        out[0] = flat[pl.ds(r, f, stride=rows), :].astype(jnp.bfloat16)


def edges(frames):
    n, bands, rows, cols = frames.shape
    group = min(8, rows)
    fb = n // 2
    block = (fb, 1, group, cols)
    out = pl.BlockSpec((1, fb, cols), lambda b, i: (b, i, 0))
    shape = jax.ShapeDtypeStruct((bands, n, cols), jnp.bfloat16)
    return pl.pallas_call(
        edge_kernel,
        grid=(bands, n // fb),
        in_specs=[
            pl.BlockSpec(block, lambda b, i: (i, b, 0, 0)),
            pl.BlockSpec(block, lambda b, i: (i, b, rows // group - 1, 0)),
        ],
        out_specs=[out, out],
        out_shape=[shape, shape],
        name="edges",
    )(frames, frames)


def shift_kernel(beta_ref, x_ref, lo_ref, hi_ref, d_ref, s0_ref, s1_ref, own_ref, sum_ref, cs):
    f, bands, rows, cols = x_ref.shape
    flat = x_ref.reshape(f * bands * rows, cols)
    steps = d_ref[...]

    def share(v):
        return jnp.broadcast_to(v.astype(jnp.float32) * 0.125, (f, cols))

    lane = lax.broadcasted_iota(jnp.int32, (f, cols), 1)
    by_row, by_col = steps[:, 0:1], steps[:, 1:2]
    up, down = share(jnp.maximum(by_row, 0)), share(jnp.maximum(-by_row, 0))
    cs[0], cs[1], cs[2] = 1.0 - up - down, up, down
    up, down = share(jnp.maximum(by_col, 0)), share(jnp.maximum(-by_col, 0))
    cs[3] = 1.0 - up - down
    cs[4] = jnp.where(lane == cols - 1, 0.0, up)
    cs[5] = jnp.where(lane == 0, 0.0, down)

    @pl.when(pl.program_id(0) == 0)
    def _():
        sum_ref[...] = jnp.zeros_like(sum_ref)

    for band, s_ref in ((0, s0_ref), (1, s1_ref)):

        def row(r):
            if r < 0:
                return lo_ref[band].astype(jnp.float32)
            if r >= rows:
                return hi_ref[band].astype(jnp.float32)
            return flat[pl.ds(band * rows + r, f, stride=bands * rows), :]

        before, here = row(-1), row(0)
        for r in range(rows):
            after = row(r + 1)
            p = cs[0] * here + cs[1] * after + cs[2] * before
            s = cs[3] * p + cs[4] * pltpu.roll(p, cols - 1, 1) + cs[5] * pltpu.roll(p, 1, 1)
            s = s.astype(jnp.bfloat16)
            s_ref[:, r * cols : (r + 1) * cols] = s
            part = jnp.sum(s.astype(jnp.float32).reshape(f // 8, 8, cols), axis=0)
            sum_ref[band, r * 8 : r * 8 + 8, :] += part
            before, here = here, after

        @pl.when(beta_ref[0] == band)
        def _():
            own_ref[...] = s_ref[...]


def shift(beta, frames, lo, hi, drift, start, count):
    _, bands, rows, cols = frames.shape
    fb = count
    while fb > 64 and fb % 2 == 0:
        fb //= 2
    first = start // fb
    edge = pl.BlockSpec((bands, fb, cols), lambda i, _: (0, i + first, 0))
    out = pl.BlockSpec((fb, rows * cols), lambda i, _: (i, 0))
    shape = jax.ShapeDtypeStruct((count, rows * cols), jnp.bfloat16)
    return pl.pallas_call(
        shift_kernel,
        grid_spec=pltpu.PrefetchScalarGridSpec(
            num_scalar_prefetch=1,
            grid=(count // fb,),
            in_specs=[
                pl.BlockSpec((fb, bands, rows, cols), lambda i, _: (i + first, 0, 0, 0)),
                edge,
                edge,
                pl.BlockSpec((fb, 2), lambda i, _: (i + first, 0)),
            ],
            out_specs=[
                out,
                out,
                out,
                pl.BlockSpec((bands, rows * 8, cols), lambda i, _: (0, 0, 0)),
            ],
            scratch_shapes=[pltpu.VMEM((6, fb, cols), jnp.float32)],
        ),
        out_shape=[shape, shape, shape, jax.ShapeDtypeStruct((bands, rows * 8, cols), jnp.float32)],
        cost_estimate=pl.CostEstimate(
            flops=count * bands * rows * cols * 12,
            bytes_accessed=count * bands * rows * cols * 7,
            transcendentals=0,
        ),
        name="shift",
    )(beta, frames, lo, hi, drift)


def gram_kernel(extra, pieces, *refs):
    refs = list(refs)
    e_ref = refs.pop(0) if extra else None
    a_ref = refs.pop(0)
    c_refs, refs = refs[:pieces], refs[pieces:]
    x_ref = refs.pop(0) if extra else None
    o_ref, c_ref = refs
    h = c_refs[0].shape[0]
    dims = (((1,), (1,)), ((), ()))
    dot = functools.partial(lax.dot_general, dimension_numbers=dims, preferred_element_type=jnp.float32)
    first = pl.program_id(0) == 0

    @pl.when(first)
    def _():
        for i, ref in enumerate(c_refs):
            c_ref[i * h : (i + 1) * h, :] = ref[...]

    if not extra:
        o_ref[...] = dot(a_ref[...], c_ref[...])
        return

    @pl.when(first)
    def _():
        both = dot(jnp.concatenate([e_ref[...], a_ref[...]], axis=0), c_ref[...])
        x_ref[...] = both[:EXTRA]
        o_ref[...] = both[EXTRA:]

    @pl.when(jnp.logical_not(first))
    def _():
        o_ref[...] = dot(a_ref[...], c_ref[...])


def gram(rows, start, count, pieces, extra=None):
    depth = rows.shape[1]
    h = pieces[0].shape[0]
    width = h * len(pieces)
    tile = 256
    while count % tile or start % tile:
        tile //= 2
    first = start // tile
    fixed = lambda shape: pl.BlockSpec(shape, lambda i: (0, 0), pipeline_mode=pl.Buffered(1))
    in_specs = [pl.BlockSpec((tile, depth), lambda i: (i + first, 0))]
    in_specs += [fixed((h, depth)) for _ in pieces]
    out_specs = [pl.BlockSpec((tile, width), lambda i: (i, 0))]
    out_shape = [jax.ShapeDtypeStruct((count, width), jnp.float32)]
    args = [rows, *pieces]
    if extra is not None:
        in_specs.insert(0, fixed((EXTRA, depth)))
        out_specs.insert(0, pl.BlockSpec((EXTRA, width), lambda i: (0, 0)))
        out_shape.insert(0, jax.ShapeDtypeStruct((EXTRA, width), jnp.float32))
        args.insert(0, extra)
    return pl.pallas_call(
        functools.partial(gram_kernel, extra is not None, len(pieces)),
        grid=(count // tile,),
        in_specs=in_specs,
        out_specs=out_specs,
        out_shape=out_shape,
        scratch_shapes=[pltpu.VMEM((width, depth), jnp.bfloat16)],
        cost_estimate=pl.CostEstimate(
            flops=2 * count * width * depth,
            bytes_accessed=2 * depth * (count + width) + 4 * count * width,
            transcendentals=0,
        ),
        name="gram",
    )(*args)


def stage_kernel(pieces, slots_ref, *refs):
    c_refs, w_ref, o_ref = refs[:pieces], refs[pieces], refs[-1]
    for i in range(pieces):

        @pl.when(pl.program_id(0) == i)
        def _():
            o_ref[...] = (c_refs[i][...].astype(jnp.float32) * w_ref[...]).astype(jnp.bfloat16)


def stage(rows, slots, pieces, weight, total):
    height, depth = pieces[0].shape
    n = len(pieces)
    fixed = lambda shape: pl.BlockSpec(shape, lambda i, _: (0, 0), pipeline_mode=pl.Buffered(1))
    in_specs = [fixed((height, depth)) for _ in pieces] + [fixed((1, depth))]
    args = [slots, *pieces, weight]
    if rows is not None:
        in_specs.append(pl.BlockSpec(memory_space=pl.ANY))
        args.append(rows)
    return pl.pallas_call(
        functools.partial(stage_kernel, n),
        grid_spec=pltpu.PrefetchScalarGridSpec(
            num_scalar_prefetch=1,
            grid=(n,),
            in_specs=in_specs,
            out_specs=pl.BlockSpec((height, depth), lambda i, s: (s[i], 0)),
        ),
        out_shape=jax.ShapeDtypeStruct((total, depth), jnp.bfloat16),
        input_output_aliases={} if rows is None else {n + 2: 0},
        cost_estimate=pl.CostEstimate(
            flops=n * height * depth, bytes_accessed=4 * n * height * depth, transcendentals=0
        ),
        name="stage",
    )(*args)


def place_kernel(parts, info_ref, *refs):
    values, ships = refs[:parts], refs[parts : 2 * parts]
    first_ref, second_ref = refs[-2:]
    width = ships[0].shape[1]
    same, upper = info_ref[2] == 1, info_ref[3] == 1
    for i in range(parts):
        at = slice(i * width, (i + 1) * width)
        a, b = values[i][:, :width], values[i][:, width:]
        keep = jnp.where(same, a, b)
        ship = ships[i][...]
        first_ref[:, at] = jnp.where(upper, ship, keep)
        second_ref[:, at] = jnp.where(upper, keep, ship)


def place(outs, info, values, ships, total):
    count = values[0].shape[0]
    parts = len(values)
    width = ships[0].shape[1]
    tile = count // 3 if count % 24 == 0 else count
    in_specs = [pl.BlockSpec((tile, 2 * width), lambda i, _: (i, 0))] * parts
    in_specs += [pl.BlockSpec((tile, width), lambda i, _: (i, 0))] * parts
    args = [info, *values, *ships]
    aliases = {}
    if outs is not None:
        aliases = {len(args): 0, len(args) + 1: 1}
        in_specs += [pl.BlockSpec(memory_space=pl.ANY)] * 2
        args += outs
    shape = jax.ShapeDtypeStruct((count, total), jnp.float32)
    return pl.pallas_call(
        functools.partial(place_kernel, parts),
        grid_spec=pltpu.PrefetchScalarGridSpec(
            num_scalar_prefetch=1,
            grid=(count // tile,),
            in_specs=in_specs,
            out_specs=[
                pl.BlockSpec((tile, parts * width), lambda i, s: (i, s[0])),
                pl.BlockSpec((tile, parts * width), lambda i, s: (i, s[1])),
            ],
        ),
        out_shape=[shape, shape],
        input_output_aliases=aliases,
        cost_estimate=pl.CostEstimate(
            flops=4 * count * width * parts,
            bytes_accessed=18 * count * width * parts,
            transcendentals=0,
        ),
        name="place",
    )(*args)


def split(x):
    parts = []
    for _ in range(3):
        part = lax.reduce_precision(x, 8, 7)
        parts.append(part.astype(jnp.bfloat16))
        x = x - part
    pad = jnp.zeros((EXTRA - 3,) + x.shape, jnp.bfloat16)
    return jnp.concatenate([jnp.stack(parts), pad])


def per_device(frames, drift):
    local_frames, _, tile_rows, columns = frames.shape
    nt, nc, npix = (lax.axis_size(a) for a in ("trow", "tcol", "pix"))
    assert nt == 4 and nc == 4
    total_frames = local_frames * nt * nc
    pixels = tile_rows * columns
    band_pixels = pixels * npix
    t, z, pix = (lax.axis_index(a) for a in ("trow", "tcol", "pix"))
    upper = z >= 2
    at_end = (z == 0) | (z == nc - 1)
    beta = upper.astype(jnp.int32)
    height = local_frames // PIECES

    head, tail = edges(frames)
    lo = lax.ppermute(tail, "pix", [(i, i + 1) for i in range(npix - 1)])
    hi = lax.ppermute(head, "pix", [(i + 1, i) for i in range(npix - 1)])
    parts = [shift(beta[None], frames, lo, hi, drift, i * height, height) for i in range(PIECES)]
    band0, band1, own, sums = ([part[j] for part in parts] for j in range(4))

    total = sum(sums).reshape(2, tile_rows, 8, columns).sum(axis=2)
    for axis, step in (("trow", 1), ("trow", 2), ("tcol", 1), ("tcol", 2)):
        total = total + lax.ppermute(total, axis, [(i, i ^ step) for i in range(4)])
    mean = (jnp.where(upper, total[1], total[0]) / total_frames).reshape(pixels)
    weight = 1.0 / (mean * mean)

    down = [(i + 1, i) for i in range(nc - 1)]
    upward = [(i, i + 1) for i in range(nc - 1)]
    outward = [(1, 0), (2, 3)]
    down1 = [lax.ppermute(band0[i], "tcol", down) for i in range(PIECES)]
    up1 = [lax.ppermute(band1[i], "tcol", upward) for i in range(PIECES)]
    first, second, third, down2, up2 = [], [], [], [], []
    for i in range(PIECES):
        first.append(jnp.where(upper, up1[i], down1[i]))
        payload = jnp.where(z == nc - 1, band1[i], down1[i])
        down2.append(lax.ppermute(payload, "tcol", down))
        payload = jnp.where(z == 0, band0[i], up1[i])
        up2.append(lax.ppermute(payload, "tcol", upward))
    for i in range(PIECES):
        second.append(jnp.where(upper, up2[i], down2[i]))
        moved = lax.ppermute(second[i], "tcol", outward)
        third.append(jnp.where(at_end, moved, jnp.where(upper, down2[i], up2[i])))
    stream = own + first + second + third
    blocks = [[0, 1, 2, 3], [1, 2, 3, 0], [2, 1, 0, 3], [3, 2, 1, 0]]
    half = nc // 2
    table = []
    for zz in range(nc):
        for pp in range(npix):
            slots = list(blocks[zz])
            if npix == 2:
                slots = [((b // half) ^ pp) * half + b % half for b in slots]
            line = [b * PIECES + i for b in slots for i in range(PIECES)]
            for k in range(nc):
                line += [blocks[zz if band == zz // half else zz ^ half][k] for band in range(2)]
            table.append(line)
    table = jnp.array(table, jnp.int32)
    same = (t & 2) == (z & 2)
    line = lax.dynamic_slice(table, (z * npix + pix, 0), (1, table.shape[1]))[0]
    flags = jnp.stack([same, upper]).astype(jnp.int32)

    index = lambda a, b: a * nc + b
    across = [
        (index(a, b), index(a ^ 1, b)) for a in range(nt) for b in range(nc) if (a & 1) == (b & 1)
    ]
    swap = [(index(a, b), index(a ^ 2, b)) for a in range(nt) for b in range(nc)]
    source = (t & 1) == (z & 1)
    near, far = [], []
    for k, piece in enumerate(stream):
        got = lax.ppermute(piece, GRID, across)
        near.append(jnp.where(source, piece, got))
        far.append(lax.ppermute(near[-1], GRID, swap))

    rows = None
    for k in range(nc):
        at = slice(k * PIECES, (k + 1) * PIECES)
        scale, *staged, _ = lax.optimization_barrier((weight, *stream[at], far[0]))
        rows = stage(rows, line[at], staged, scale[None], nc * local_frames)
    dims = (((1,), (1,)), ((), ()))
    level = lax.dot_general(rows, split(mean), dims, preferred_element_type=jnp.float32).sum(axis=1)
    count = nc * local_frames // npix
    if npix == 2:
        level = level[:count] + lax.ppermute(level[count:], "pix", [(0, 1), (1, 0)])
    else:
        level = lax.psum_scatter(level, "pix", scatter_dimension=0, tiled=True)
    row_scale = band_pixels / level
    extra = split(1.0 / mean)

    def correlate(cols, gate):
        if npix == 2:
            sums, theirs = gram(rows, count, count, cols, extra)
            theirs = lax.ppermute(theirs, "pix", [(0, 1), (1, 0)])
            sums = sums[:3].sum(axis=0)
            sums = sums + lax.ppermute(sums, "pix", [(0, 1), (1, 0)])
            (total,) = gram(rows, 0, count, cols)
        else:
            sums, part = gram(rows, 0, nc * local_frames, cols, extra)
            sums = lax.psum(sums[:3].sum(axis=0), "pix")
            total = lax.psum_scatter(part, "pix", scatter_dimension=0, tiled=True)
            theirs = jnp.zeros_like(total)
        theirs, gate = lax.optimization_barrier((theirs, gate))
        return (total + theirs) * row_scale[:, None] * (1.0 / sums)[None, :]

    over = [(i, i ^ 2) for i in range(nc)]
    chunks = [[(k, 0, PIECES)] for k in range(nc - 1)] + [[(nc - 1, i, 1) for i in range(PIECES)]]
    gate, outs, n = row_scale, None, 0
    for parts in chunks:
        values, ships = [], []
        for k, i, size in parts:
            lo = k * PIECES + i
            value = correlate(near[lo : lo + size] + far[lo : lo + size], gate)
            a, b = value[:, : size * height], value[:, size * height :]
            gate = (jnp.where(same, b, a) - 1.0).astype(SHIP)
            values.append(value)
            ships.append(lax.ppermute(gate, "tcol", over).astype(jnp.float32) + 1.0)
            n += 1
        at = nc * PIECES + 2 * k
        info = jnp.concatenate([line[at : at + 2], flags])
        outs = place(outs, info, values, ships, nc * local_frames)
    return outs[0], outs[1]


def solution(mesh):
    in_specs = (P(("trow", "tcol"), None, "pix", None), P(("trow", "tcol"), None))
    out_specs = (P(("trow", "pix"), "tcol"), P(("trow", "pix"), "tcol"))

    return jax.shard_map(
        per_device, mesh=mesh, in_specs=in_specs, out_specs=out_specs, check_vma=False
    )
```

```python
import functools

import jax
import jax.numpy as jnp
from jax import lax
from jax.experimental import pallas as pl
from jax.experimental.pallas import tpu as pltpu
from jax.sharding import PartitionSpec as P


PIECES = 2
SHIP = jnp.float16
EXTRA = 16
GRID = ("trow", "tcol")


def edge_kernel(first_ref, last_ref, head_ref, tail_ref):
    f, rows, cols = first_ref.shape[0], first_ref.shape[2], first_ref.shape[3]
    for ref, out, r in ((first_ref, head_ref, 0), (last_ref, tail_ref, rows - 1)):
        flat = ref.reshape(f * rows, cols)
        out[0] = flat[pl.ds(r, f, stride=rows), :].astype(jnp.bfloat16)


def edges(frames):
    n, bands, rows, cols = frames.shape
    group = min(8, rows)
    fb = n // 2
    block = (fb, 1, group, cols)
    out = pl.BlockSpec((1, fb, cols), lambda b, i: (b, i, 0))
    shape = jax.ShapeDtypeStruct((bands, n, cols), jnp.bfloat16)
    return pl.pallas_call(
        edge_kernel,
        grid=(bands, n // fb),
        in_specs=[
            pl.BlockSpec(block, lambda b, i: (i, b, 0, 0)),
            pl.BlockSpec(block, lambda b, i: (i, b, rows // group - 1, 0)),
        ],
        out_specs=[out, out],
        out_shape=[shape, shape],
        name="edges",
    )(frames, frames)


def shift_kernel(beta_ref, x_ref, lo_ref, hi_ref, d_ref, s0_ref, s1_ref, own_ref, sum_ref, cs):
    f, bands, rows, cols = x_ref.shape
    flat = x_ref.reshape(f * bands * rows, cols)
    steps = d_ref[...]

    def share(v):
        return jnp.broadcast_to(v.astype(jnp.float32) * 0.125, (f, cols))

    lane = lax.broadcasted_iota(jnp.int32, (f, cols), 1)
    by_row, by_col = steps[:, 0:1], steps[:, 1:2]
    up, down = share(jnp.maximum(by_row, 0)), share(jnp.maximum(-by_row, 0))
    cs[0], cs[1], cs[2] = 1.0 - up - down, up, down
    up, down = share(jnp.maximum(by_col, 0)), share(jnp.maximum(-by_col, 0))
    cs[3] = 1.0 - up - down
    cs[4] = jnp.where(lane == cols - 1, 0.0, up)
    cs[5] = jnp.where(lane == 0, 0.0, down)

    @pl.when(pl.program_id(0) == 0)
    def _():
        sum_ref[...] = jnp.zeros_like(sum_ref)

    for band, s_ref in ((0, s0_ref), (1, s1_ref)):

        def load(r):
            return flat[pl.ds(band * rows + r, f, stride=bands * rows), :]

        last = hi_ref[band].astype(jnp.float32)
        unroll = 4 if rows % 4 == 0 else 1

        def body(q, carry):
            before, here = carry
            for u in range(unroll):
                r = q * unroll + u
                after = load(jnp.minimum(r + 1, rows - 1))
                if u == unroll - 1:
                    after = jnp.where(r == rows - 1, last, after)
                p = cs[0] * here + cs[1] * after + cs[2] * before
                s = cs[3] * p + cs[4] * pltpu.roll(p, cols - 1, 1) + cs[5] * pltpu.roll(p, 1, 1)
                s = s.astype(jnp.bfloat16)
                s_ref[:, pl.ds(pl.multiple_of(r * cols, cols), cols)] = s
                part = jnp.sum(s.astype(jnp.float32).reshape(f // 8, 8, cols), axis=0)
                sum_ref[band, pl.ds(pl.multiple_of(r * 8, 8), 8), :] += part
                before, here = here, after
            return before, here

        lax.fori_loop(0, rows // unroll, body, (lo_ref[band].astype(jnp.float32), load(0)))

        @pl.when(beta_ref[0] == band)
        def _():
            own_ref[...] = s_ref[...]


def shift(beta, frames, lo, hi, drift, start, count):
    _, bands, rows, cols = frames.shape
    fb = count
    while fb > 64 and fb % 2 == 0:
        fb //= 2
    first = start // fb
    edge = pl.BlockSpec((bands, fb, cols), lambda i, _: (0, i + first, 0))
    out = pl.BlockSpec((fb, rows * cols), lambda i, _: (i, 0))
    shape = jax.ShapeDtypeStruct((count, rows * cols), jnp.bfloat16)
    return pl.pallas_call(
        shift_kernel,
        grid_spec=pltpu.PrefetchScalarGridSpec(
            num_scalar_prefetch=1,
            grid=(count // fb,),
            in_specs=[
                pl.BlockSpec((fb, bands, rows, cols), lambda i, _: (i + first, 0, 0, 0)),
                edge,
                edge,
                pl.BlockSpec((fb, 2), lambda i, _: (i + first, 0)),
            ],
            out_specs=[
                out,
                out,
                out,
                pl.BlockSpec((bands, rows * 8, cols), lambda i, _: (0, 0, 0)),
            ],
            scratch_shapes=[pltpu.VMEM((6, fb, cols), jnp.float32)],
        ),
        out_shape=[shape, shape, shape, jax.ShapeDtypeStruct((bands, rows * 8, cols), jnp.float32)],
        cost_estimate=pl.CostEstimate(
            flops=count * bands * rows * cols * 12,
            bytes_accessed=count * bands * rows * cols * 7,
            transcendentals=0,
        ),
        name="shift",
    )(beta, frames, lo, hi, drift)


def gram_kernel(extra, pieces, slots_ref, *refs):
    refs = list(refs)
    e_ref = refs.pop(0) if extra else None
    a_ref = refs.pop(0)
    c_refs = refs[:pieces]
    o_ref, c_ref = refs[-2:]

    @pl.when(pl.program_id(0) == 0)
    def _():
        at = 0
        for ref in c_refs:
            c_ref[at : at + ref.shape[0], :] = ref[...]
            at += ref.shape[0]

    a = a_ref[...]
    if extra:
        a = jnp.concatenate([e_ref[...], a], axis=0)
    width = o_ref.shape[1]
    step = 256 if width % 256 == 0 else 128

    @pl.loop(0, width // step)
    def _(j):
        at = pl.ds(pl.multiple_of(j * step, step), step)
        part = lax.dot_general(
            a, c_ref[at, :], (((1,), (1,)), ((), ())), preferred_element_type=jnp.float32
        )
        if extra:
            refs[-3][:, at] = part[:EXTRA]
            part = part[EXTRA:]
        o_ref[:, at] = part


def gram(rows, blocks, slots, total, pieces, extra=None, prev=None):
    depth = rows.shape[1]
    height = rows.shape[0] // blocks
    n = slots.shape[1]
    width = sum(p.shape[0] for p in pieces)
    fixed = lambda shape: pl.BlockSpec(shape, lambda i, s: (0, 0), pipeline_mode=pl.Buffered(1))
    in_specs = [pl.BlockSpec((height, depth), lambda i, s: (s[0, i], 0))]
    in_specs += [fixed(p.shape) for p in pieces]
    out_specs = [pl.BlockSpec((height, width), lambda i, s: (s[1, i], 0))]
    out_shape = [jax.ShapeDtypeStruct((total * height, width), jnp.float32)]
    args = [rows, *pieces]
    if extra is not None:
        in_specs.insert(0, fixed((EXTRA, depth)))
        out_specs.insert(0, pl.BlockSpec((EXTRA, width), lambda i, s: (0, 0)))
        out_shape.insert(0, jax.ShapeDtypeStruct((EXTRA, width), jnp.float32))
        args.insert(0, extra)
    aliases = {}
    if prev is not None:
        in_specs.append(pl.BlockSpec(memory_space=pl.ANY))
        aliases = {len(args) + 1: 0}
        args.append(prev)
    return pl.pallas_call(
        functools.partial(gram_kernel, extra is not None, len(pieces)),
        grid_spec=pltpu.PrefetchScalarGridSpec(
            num_scalar_prefetch=1,
            grid=(n,),
            in_specs=in_specs,
            out_specs=out_specs,
            scratch_shapes=[pltpu.VMEM((width, depth), jnp.bfloat16)],
        ),
        out_shape=out_shape,
        input_output_aliases=aliases,
        cost_estimate=pl.CostEstimate(
            flops=2 * n * height * width * depth,
            bytes_accessed=2 * depth * (n * height + width) + 4 * n * height * width,
            transcendentals=0,
        ),
        name="gram",
    )(slots, *args)


def stage_kernel(pieces, slots_ref, *refs):
    c_refs, w_ref, m_ref = refs[:pieces], refs[pieces], refs[pieces + 1]
    o_ref, l_ref = refs[-2:]
    lanes = l_ref.shape[1]
    for i in range(pieces):

        @pl.when(pl.program_id(0) == i)
        def _():

            def body(c, level):
                at = pl.ds(pl.multiple_of(c * lanes, lanes), lanes)
                value = c_refs[i][:, at].astype(jnp.float32) * w_ref[:, at]
                value = value.astype(jnp.bfloat16)
                o_ref[:, at] = value
                return level + value.astype(jnp.float32) * m_ref[:, at]

            chunks = o_ref.shape[1] // lanes
            level = lax.fori_loop(0, chunks, body, jnp.zeros(l_ref.shape, jnp.float32))
            l_ref[...] = level


def stage(prev, slots, pieces, weight, mean, total):
    height, depth = pieces[0].shape
    n = len(pieces)
    lanes = min(128, depth)
    fixed = lambda shape: pl.BlockSpec(shape, lambda i, _: (0, 0), pipeline_mode=pl.Buffered(1))
    in_specs = [fixed((height, depth)) for _ in pieces] + [fixed((1, depth))] * 2
    args = [slots, *pieces, weight, mean]
    aliases = {}
    if prev is not None:
        aliases = {len(args): 0, len(args) + 1: 1}
        in_specs += [pl.BlockSpec(memory_space=pl.ANY)] * 2
        args += prev
    return pl.pallas_call(
        functools.partial(stage_kernel, n),
        grid_spec=pltpu.PrefetchScalarGridSpec(
            num_scalar_prefetch=1,
            grid=(n,),
            in_specs=in_specs,
            out_specs=[
                pl.BlockSpec((height, depth), lambda i, s: (s[i], 0)),
                pl.BlockSpec((height, lanes), lambda i, s: (s[i], 0)),
            ],
        ),
        out_shape=[
            jax.ShapeDtypeStruct((total, depth), jnp.bfloat16),
            jax.ShapeDtypeStruct((total, lanes), jnp.float32),
        ],
        input_output_aliases=aliases,
        cost_estimate=pl.CostEstimate(
            flops=n * height * depth, bytes_accessed=4 * n * height * depth, transcendentals=0
        ),
        name="stage",
    )(*args)


def place_kernel(parts, info_ref, *refs):
    values, ships = refs[:parts], refs[parts : 2 * parts]
    first_ref, second_ref = refs[-2:]
    width = ships[0].shape[1]
    same, upper = info_ref[2] == 1, info_ref[3] == 1
    for i in range(parts):
        at = slice(i * width, (i + 1) * width)
        a, b = values[i][:, :width], values[i][:, width:]
        keep = jnp.where(same, a, b)
        ship = ships[i][...]
        first_ref[:, at] = jnp.where(upper, ship, keep)
        second_ref[:, at] = jnp.where(upper, keep, ship)


def place(outs, info, values, ships, total):
    count = values[0].shape[0]
    parts = len(values)
    width = ships[0].shape[1]
    tile = count // 3 if count % 24 == 0 else count
    in_specs = [pl.BlockSpec((tile, 2 * width), lambda i, _: (i, 0))] * parts
    in_specs += [pl.BlockSpec((tile, width), lambda i, _: (i, 0))] * parts
    args = [info, *values, *ships]
    aliases = {}
    if outs is not None:
        aliases = {len(args): 0, len(args) + 1: 1}
        in_specs += [pl.BlockSpec(memory_space=pl.ANY)] * 2
        args += outs
    shape = jax.ShapeDtypeStruct((count, total), jnp.float32)
    return pl.pallas_call(
        functools.partial(place_kernel, parts),
        grid_spec=pltpu.PrefetchScalarGridSpec(
            num_scalar_prefetch=1,
            grid=(count // tile,),
            in_specs=in_specs,
            out_specs=[
                pl.BlockSpec((tile, parts * width), lambda i, s: (i, s[0])),
                pl.BlockSpec((tile, parts * width), lambda i, s: (i, s[1])),
            ],
        ),
        out_shape=[shape, shape],
        input_output_aliases=aliases,
        cost_estimate=pl.CostEstimate(
            flops=4 * count * width * parts,
            bytes_accessed=18 * count * width * parts,
            transcendentals=0,
        ),
        name="place",
    )(*args)


def split(x):
    parts = []
    for _ in range(3):
        part = lax.reduce_precision(x, 8, 7)
        parts.append(part.astype(jnp.bfloat16))
        x = x - part
    pad = jnp.zeros((EXTRA - 3,) + x.shape, jnp.bfloat16)
    return jnp.concatenate([jnp.stack(parts), pad])


def per_device(frames, drift):
    local_frames, _, tile_rows, columns = frames.shape
    nt, nc, npix = (lax.axis_size(a) for a in ("trow", "tcol", "pix"))
    assert nt == 4 and nc == 4
    total_frames = local_frames * nt * nc
    pixels = tile_rows * columns
    band_pixels = pixels * npix
    t, z, pix = (lax.axis_index(a) for a in ("trow", "tcol", "pix"))
    upper = z >= 2
    at_end = (z == 0) | (z == nc - 1)
    beta = upper.astype(jnp.int32)
    height = local_frames // PIECES

    head, tail = edges(frames)
    lo = lax.ppermute(tail, "pix", [(i, i + 1) for i in range(npix - 1)])
    hi = lax.ppermute(head, "pix", [(i + 1, i) for i in range(npix - 1)])
    parts = [shift(beta[None], frames, lo, hi, drift, i * height, height) for i in range(PIECES)]
    band0, band1, own, sums = ([part[j] for part in parts] for j in range(4))

    total = sum(sums).reshape(2, tile_rows, 8, columns).sum(axis=2)
    for axis, step in (("trow", 1), ("trow", 2), ("tcol", 1), ("tcol", 2)):
        total = total + lax.ppermute(total, axis, [(i, i ^ step) for i in range(4)])
    mean = (jnp.where(upper, total[1], total[0]) / total_frames).reshape(pixels)
    weight = 1.0 / (mean * mean)

    down = [(i + 1, i) for i in range(nc - 1)]
    upward = [(i, i + 1) for i in range(nc - 1)]
    outward = [(1, 0), (2, 3)]
    down1 = [lax.ppermute(band0[i], "tcol", down) for i in range(PIECES)]
    up1 = [lax.ppermute(band1[i], "tcol", upward) for i in range(PIECES)]
    first, second, third, down2, up2 = [], [], [], [], []
    for i in range(PIECES):
        first.append(jnp.where(upper, up1[i], down1[i]))
        payload = jnp.where(z == nc - 1, band1[i], down1[i])
        down2.append(lax.ppermute(payload, "tcol", down))
        payload = jnp.where(z == 0, band0[i], up1[i])
        up2.append(lax.ppermute(payload, "tcol", upward))
    for i in range(PIECES):
        second.append(jnp.where(upper, up2[i], down2[i]))
        moved = lax.ppermute(second[i], "tcol", outward)
        third.append(jnp.where(at_end, moved, jnp.where(upper, down2[i], up2[i])))
    stream = own + first + second + third
    blocks = [[0, 1, 2, 3], [1, 2, 3, 0], [2, 1, 0, 3], [3, 2, 1, 0]]
    half = nc // 2
    table = []
    for zz in range(nc):
        for pp in range(npix):
            slots = list(blocks[zz])
            if npix == 2:
                slots = [((b // half) ^ pp) * half + b % half for b in slots]
            line = [b * PIECES + i for b in slots for i in range(PIECES)] + slots
            for k in range(nc):
                line += [blocks[zz if band == zz // half else zz ^ half][k] for band in range(2)]
            table.append(line)
    table = jnp.array(table, jnp.int32)
    same = (t & 2) == (z & 2)
    line = lax.dynamic_slice(table, (z * npix + pix, 0), (1, table.shape[1]))[0]
    flags = jnp.stack([same, upper]).astype(jnp.int32)

    index = lambda a, b: a * nc + b
    across = [
        (index(a, b), index(a ^ 1, b)) for a in range(nt) for b in range(nc) if (a & 1) == (b & 1)
    ]
    swap = [(index(a, b), index(a ^ 2, b)) for a in range(nt) for b in range(nc)]
    source = (t & 1) == (z & 1)
    near, far = [], []
    for k, piece in enumerate(stream):
        got = lax.ppermute(piece, GRID, across)
        near.append(jnp.where(source, piece, got))
        far.append(lax.ppermute(near[-1], GRID, swap))

    staged = None
    for k in range(nc):
        at = slice(k * PIECES, (k + 1) * PIECES)
        scale, *block, _ = lax.optimization_barrier((weight, *stream[at], far[0]))
        staged = stage(staged, line[at], block, scale[None], mean[None], nc * local_frames)
        if k == nc - 2:
            early = staged[0]
    rows, level = staged
    level = level.sum(axis=1)
    count = nc * local_frames // npix
    if npix == 2:
        level = level[:count] + lax.ppermute(level[count:], "pix", [(0, 1), (1, 0)])
    else:
        level = lax.psum_scatter(level, "pix", scatter_dimension=0, tiled=True)
    row_scale = band_pixels / level
    extra = split(1.0 / mean)
    order = line[nc * PIECES : nc * PIECES + nc]
    order = jnp.stack([order, order])
    mine_slots = jnp.array([range(half), range(half)], jnp.int32)
    their_slots = jnp.array([range(half, nc), range(half)], jnp.int32)
    all_slots = jnp.array([range(nc), range(nc)], jnp.int32)

    def correlate(cols, gate, ahead):
        other_core = [(0, 1), (1, 0)]
        if npix == 2 and ahead:
            sums, part = gram(early, nc, order[:, : nc - 1], nc, cols, extra)
            (part,) = gram(rows, nc, order[:, nc - 1 :], nc, cols, prev=part)
            total, theirs = part[:count], lax.ppermute(part[count:], "pix", other_core)
        elif npix == 2:
            sums, theirs = gram(rows, nc, their_slots, half, cols, extra)
            theirs = lax.ppermute(theirs, "pix", other_core)
            (total,) = gram(rows, nc, mine_slots, half, cols)
        else:
            sums, part = gram(rows, nc, all_slots, nc, cols, extra)
            total = lax.psum_scatter(part, "pix", scatter_dimension=0, tiled=True)
            theirs = jnp.zeros_like(total)
        sums = sums[:3].sum(axis=0)
        if npix == 2:
            sums = sums + lax.ppermute(sums, "pix", other_core)
        else:
            sums = lax.psum(sums, "pix")
        theirs, gate = lax.optimization_barrier((theirs, gate))
        return (total + theirs) * row_scale[:, None] * (1.0 / sums)[None, :]

    over = [(i, i ^ 2) for i in range(nc)]
    chunks = [[(k, 0, PIECES)] for k in range(nc - 1)] + [[(nc - 1, i, 1) for i in range(PIECES)]]
    gate, outs, n = row_scale, None, 0
    for parts in chunks:
        values, ships = [], []
        for k, i, size in parts:
            lo = k * PIECES + i
            value = correlate(near[lo : lo + size] + far[lo : lo + size], gate, k < 2)
            a, b = value[:, : size * height], value[:, size * height :]
            gate = (jnp.where(same, b, a) - 1.0).astype(SHIP)
            values.append(value)
            ships.append(lax.ppermute(gate, "tcol", over).astype(jnp.float32) + 1.0)
            n += 1
        at = nc * PIECES + nc + 2 * k
        info = jnp.concatenate([line[at : at + 2], flags])
        outs = place(outs, info, values, ships, nc * local_frames)
    return outs[0], outs[1]


def solution(mesh):
    in_specs = (P(("trow", "tcol"), None, "pix", None), P(("trow", "tcol"), None))
    out_specs = (P(("trow", "pix"), "tcol"), P(("trow", "pix"), "tcol"))

    return jax.shard_map(
        per_device, mesh=mesh, in_specs=in_specs, out_specs=out_specs, check_vma=False
    )
```

```python
import functools

import jax
import jax.numpy as jnp
from jax import lax
from jax.experimental import pallas as pl
from jax.experimental.pallas import tpu as pltpu
from jax.sharding import PartitionSpec as P


PIECES = 2
SHIP = jnp.float16
EXTRA = 16
GRID = ("trow", "tcol")


def edge_kernel(first_ref, last_ref, head_ref, tail_ref):
    f, rows, cols = first_ref.shape[0], first_ref.shape[2], first_ref.shape[3]
    for ref, out, r in ((first_ref, head_ref, 0), (last_ref, tail_ref, rows - 1)):
        flat = ref.reshape(f * rows, cols)
        out[0] = flat[pl.ds(r, f, stride=rows), :].astype(jnp.bfloat16)


def edges(frames, start, n):
    _, bands, rows, cols = frames.shape
    group = min(8, rows)
    fb = n
    first = start // fb
    block = (fb, 1, group, cols)
    out = pl.BlockSpec((1, fb, cols), lambda b, i: (b, i, 0))
    shape = jax.ShapeDtypeStruct((bands, n, cols), jnp.bfloat16)
    return pl.pallas_call(
        edge_kernel,
        grid=(bands, n // fb),
        in_specs=[
            pl.BlockSpec(block, lambda b, i: (i + first, b, 0, 0)),
            pl.BlockSpec(block, lambda b, i: (i + first, b, rows // group - 1, 0)),
        ],
        out_specs=[out, out],
        out_shape=[shape, shape],
        name="edges",
    )(frames, frames)


def shift_kernel(unroll, beta_ref, x_ref, lo_ref, hi_ref, d_ref, s0_ref, s1_ref, own_ref, sum_ref, cs):
    f, bands, rows, cols = x_ref.shape
    flat = x_ref.reshape(f * bands * rows, cols)
    steps = d_ref[...]

    def share(v):
        return jnp.broadcast_to(v.astype(jnp.float32) * 0.125, (f, cols))

    lane = lax.broadcasted_iota(jnp.int32, (f, cols), 1)
    by_row, by_col = steps[:, 0:1], steps[:, 1:2]
    up, down = share(jnp.maximum(by_row, 0)), share(jnp.maximum(-by_row, 0))
    cs[0], cs[1], cs[2] = 1.0 - up - down, up, down
    up, down = share(jnp.maximum(by_col, 0)), share(jnp.maximum(-by_col, 0))
    cs[3] = 1.0 - up - down
    cs[4] = jnp.where(lane == cols - 1, 0.0, up)
    cs[5] = jnp.where(lane == 0, 0.0, down)

    @pl.when(pl.program_id(0) == 0)
    def _():
        sum_ref[...] = jnp.zeros_like(sum_ref)

    for band, s_ref in ((0, s0_ref), (1, s1_ref)):

        def load(r):
            return flat[pl.ds(band * rows + r, f, stride=bands * rows), :]

        first, last = lo_ref[band].astype(jnp.float32), hi_ref[band].astype(jnp.float32)

        def store(before, here, after, pixels, partial):
            p = cs[0] * here + cs[1] * after + cs[2] * before
            s = cs[3] * p + cs[4] * pltpu.roll(p, cols - 1, 1) + cs[5] * pltpu.roll(p, 1, 1)
            s = s.astype(jnp.bfloat16)
            s_ref[:, pixels] = s
            sum_ref[band, partial, :] += jnp.sum(s.astype(jnp.float32).reshape(f // 8, 8, cols), axis=0)

        def body(q, carry):
            before, here = carry
            for u in range(unroll):
                r = q * unroll + u
                after = load(jnp.minimum(r + 1, rows - 1))
                if u == unroll - 1:
                    after = jnp.where(r == rows - 1, last, after)
                pixels = pl.ds(pl.multiple_of(r * cols, cols), cols)
                store(before, here, after, pixels, pl.ds(pl.multiple_of(r * 8, 8), 8))
                before, here = here, after
            return before, here

        if unroll < rows:
            lax.fori_loop(0, rows // unroll, body, (first, load(0)))
        else:
            before, here = first, load(0)
            for r in range(rows):
                after = load(r + 1) if r + 1 < rows else last
                store(before, here, after, slice(r * cols, (r + 1) * cols), slice(r * 8, r * 8 + 8))
                before, here = here, after

        @pl.when(beta_ref[0] == band)
        def _():
            own_ref[...] = s_ref[...]


def shift(beta, frames, lo, hi, drift, start, count, unroll):
    _, bands, rows, cols = frames.shape
    fb = count
    while fb > 64 and fb % 2 == 0:
        fb //= 2
    first = start // fb
    edge = pl.BlockSpec((bands, fb, cols), lambda i, _: (0, i, 0))
    out = pl.BlockSpec((fb, rows * cols), lambda i, _: (i, 0))
    shape = jax.ShapeDtypeStruct((count, rows * cols), jnp.bfloat16)
    return pl.pallas_call(
        functools.partial(shift_kernel, unroll if rows % unroll == 0 else rows),
        grid_spec=pltpu.PrefetchScalarGridSpec(
            num_scalar_prefetch=1,
            grid=(count // fb,),
            in_specs=[
                pl.BlockSpec((fb, bands, rows, cols), lambda i, _: (i + first, 0, 0, 0)),
                edge,
                edge,
                pl.BlockSpec((fb, 2), lambda i, _: (i + first, 0)),
            ],
            out_specs=[
                out,
                out,
                out,
                pl.BlockSpec((bands, rows * 8, cols), lambda i, _: (0, 0, 0)),
            ],
            scratch_shapes=[pltpu.VMEM((6, fb, cols), jnp.float32)],
        ),
        out_shape=[shape, shape, shape, jax.ShapeDtypeStruct((bands, rows * 8, cols), jnp.float32)],
        cost_estimate=pl.CostEstimate(
            flops=count * bands * rows * cols * 12,
            bytes_accessed=count * bands * rows * cols * 7,
            transcendentals=0,
        ),
        name="shift",
    )(beta, frames, lo, hi, drift)


def gram_kernel(extra, step, pieces, slots_ref, *refs):
    refs = list(refs)
    e_ref = refs.pop(0) if extra else None
    a_ref = refs.pop(0)
    c_refs = refs[:pieces]
    o_ref, c_ref = refs[-2:]

    @pl.when(pl.program_id(0) == 0)
    def _():
        at = 0
        for ref in c_refs:
            c_ref[at : at + ref.shape[0], :] = ref[...]
            at += ref.shape[0]

    a = a_ref[...]
    if extra:
        a = jnp.concatenate([e_ref[...], a], axis=0)
    width = o_ref.shape[1]

    def chunk(at):
        part = lax.dot_general(
            a, c_ref[at, :], (((1,), (1,)), ((), ())), preferred_element_type=jnp.float32
        )
        if extra:
            refs[-3][:, at] = part[:EXTRA]
            part = part[EXTRA:]
        o_ref[:, at] = part

    if step < width and width % step == 0:

        @pl.loop(0, width // step)
        def _(j):
            chunk(pl.ds(pl.multiple_of(j * step, step), step))

    else:
        chunk(slice(0, width))


def gram(rows, height, slots, total, pieces, extra=None, prev=None, step=1024):
    depth = rows.shape[1]
    n = slots.shape[1]
    width = sum(p.shape[0] for p in pieces)
    fixed = lambda shape: pl.BlockSpec(shape, lambda i, s: (0, 0), pipeline_mode=pl.Buffered(1))
    in_specs = [pl.BlockSpec((height, depth), lambda i, s: (s[0, i], 0))]
    in_specs += [fixed(p.shape) for p in pieces]
    out_specs = [pl.BlockSpec((height, width), lambda i, s: (s[1, i], 0))]
    out_shape = [jax.ShapeDtypeStruct((total * height, width), jnp.float32)]
    args = [rows, *pieces]
    if extra is not None:
        in_specs.insert(0, fixed((EXTRA, depth)))
        out_specs.insert(0, pl.BlockSpec((EXTRA, width), lambda i, s: (0, 0)))
        out_shape.insert(0, jax.ShapeDtypeStruct((EXTRA, width), jnp.float32))
        args.insert(0, extra)
    aliases = {}
    if prev is not None:
        in_specs.append(pl.BlockSpec(memory_space=pl.ANY))
        aliases = {len(args) + 1: 0}
        args.append(prev)
    return pl.pallas_call(
        functools.partial(gram_kernel, extra is not None, step, len(pieces)),
        grid_spec=pltpu.PrefetchScalarGridSpec(
            num_scalar_prefetch=1,
            grid=(n,),
            in_specs=in_specs,
            out_specs=out_specs,
            scratch_shapes=[pltpu.VMEM((width, depth), jnp.bfloat16)],
        ),
        out_shape=out_shape,
        input_output_aliases=aliases,
        cost_estimate=pl.CostEstimate(
            flops=2 * n * height * width * depth,
            bytes_accessed=2 * depth * (n * height + width) + 4 * n * height * width,
            transcendentals=0,
        ),
        name="gram",
    )(slots, *args)


def stage_kernel(pieces, slots_ref, *refs):
    c_refs, w_ref, m_ref = refs[:pieces], refs[pieces], refs[pieces + 1]
    o_ref, l_ref = refs[-2:]
    lanes = l_ref.shape[1]
    for i in range(pieces):

        @pl.when(pl.program_id(0) == i)
        def _():

            def body(c, level):
                at = pl.ds(pl.multiple_of(c * lanes, lanes), lanes)
                value = c_refs[i][:, at].astype(jnp.float32) * w_ref[:, at]
                value = value.astype(jnp.bfloat16)
                o_ref[:, at] = value
                return level + value.astype(jnp.float32) * m_ref[:, at]

            chunks = o_ref.shape[1] // lanes
            level = lax.fori_loop(0, chunks, body, jnp.zeros(l_ref.shape, jnp.float32))
            l_ref[...] = level


def stage(prev, slots, pieces, weight, mean, total):
    height, depth = pieces[0].shape
    n = len(pieces)
    lanes = min(128, depth)
    fixed = lambda shape: pl.BlockSpec(shape, lambda i, _: (0, 0), pipeline_mode=pl.Buffered(1))
    in_specs = [fixed((height, depth)) for _ in pieces] + [fixed((1, depth))] * 2
    args = [slots, *pieces, weight, mean]
    aliases = {}
    if prev is not None:
        aliases = {len(args): 0, len(args) + 1: 1}
        in_specs += [pl.BlockSpec(memory_space=pl.ANY)] * 2
        args += prev
    return pl.pallas_call(
        functools.partial(stage_kernel, n),
        grid_spec=pltpu.PrefetchScalarGridSpec(
            num_scalar_prefetch=1,
            grid=(n,),
            in_specs=in_specs,
            out_specs=[
                pl.BlockSpec((height, depth), lambda i, s: (s[i], 0)),
                pl.BlockSpec((height, lanes), lambda i, s: (s[i], 0)),
            ],
        ),
        out_shape=[
            jax.ShapeDtypeStruct((total, depth), jnp.bfloat16),
            jax.ShapeDtypeStruct((total, lanes), jnp.float32),
        ],
        input_output_aliases=aliases,
        cost_estimate=pl.CostEstimate(
            flops=n * height * depth, bytes_accessed=4 * n * height * depth, transcendentals=0
        ),
        name="stage",
    )(*args)


def place_kernel(parts, info_ref, *refs):
    values, ships = refs[:parts], refs[parts : 2 * parts]
    first_ref, second_ref = refs[-2:]
    width = ships[0].shape[1]
    same, upper = info_ref[2] == 1, info_ref[3] == 1
    for i in range(parts):
        at = slice(i * width, (i + 1) * width)
        a, b = values[i][:, :width], values[i][:, width:]
        keep = jnp.where(same, a, b)
        ship = ships[i][...]
        first_ref[:, at] = jnp.where(upper, ship, keep)
        second_ref[:, at] = jnp.where(upper, keep, ship)


def place(outs, info, values, ships, total):
    count = values[0].shape[0]
    parts = len(values)
    width = ships[0].shape[1]
    tile = count // 3 if count % 24 == 0 else count
    in_specs = [pl.BlockSpec((tile, 2 * width), lambda i, _: (i, 0))] * parts
    in_specs += [pl.BlockSpec((tile, width), lambda i, _: (i, 0))] * parts
    args = [info, *values, *ships]
    aliases = {}
    if outs is not None:
        aliases = {len(args): 0, len(args) + 1: 1}
        in_specs += [pl.BlockSpec(memory_space=pl.ANY)] * 2
        args += outs
    shape = jax.ShapeDtypeStruct((count, total), jnp.float32)
    return pl.pallas_call(
        functools.partial(place_kernel, parts),
        grid_spec=pltpu.PrefetchScalarGridSpec(
            num_scalar_prefetch=1,
            grid=(count // tile,),
            in_specs=in_specs,
            out_specs=[
                pl.BlockSpec((tile, parts * width), lambda i, s: (i, s[0])),
                pl.BlockSpec((tile, parts * width), lambda i, s: (i, s[1])),
            ],
        ),
        out_shape=[shape, shape],
        input_output_aliases=aliases,
        cost_estimate=pl.CostEstimate(
            flops=4 * count * width * parts,
            bytes_accessed=18 * count * width * parts,
            transcendentals=0,
        ),
        name="place",
    )(*args)


def split(x):
    parts = []
    for _ in range(3):
        part = lax.reduce_precision(x, 8, 7)
        parts.append(part.astype(jnp.bfloat16))
        x = x - part
    pad = jnp.zeros((EXTRA - 3,) + x.shape, jnp.bfloat16)
    return jnp.concatenate([jnp.stack(parts), pad])


def per_device(frames, drift):
    local_frames, _, tile_rows, columns = frames.shape
    nt, nc, npix = (lax.axis_size(a) for a in ("trow", "tcol", "pix"))
    assert nt == 4 and nc == 4
    total_frames = local_frames * nt * nc
    pixels = tile_rows * columns
    band_pixels = pixels * npix
    t, z, pix = (lax.axis_index(a) for a in ("trow", "tcol", "pix"))
    upper = z >= 2
    at_end = (z == 0) | (z == nc - 1)
    beta = upper.astype(jnp.int32)
    height = local_frames // PIECES

    parts = []
    for i in range(PIECES):
        head, tail = edges(frames, i * height, height)
        lo = lax.ppermute(tail, "pix", [(j, j + 1) for j in range(npix - 1)])
        hi = lax.ppermute(head, "pix", [(j + 1, j) for j in range(npix - 1)])
        unroll = 4 if i else tile_rows
        parts.append(shift(beta[None], frames, lo, hi, drift, i * height, height, unroll))
    band0, band1, own, sums = ([part[j] for part in parts] for j in range(4))

    total = sum(sums).reshape(2, tile_rows, 8, columns).sum(axis=2)
    for axis, step in (("trow", 1), ("trow", 2), ("tcol", 1), ("tcol", 2)):
        total = total + lax.ppermute(total, axis, [(i, i ^ step) for i in range(4)])
    mean = (jnp.where(upper, total[1], total[0]) / total_frames).reshape(pixels)
    weight = 1.0 / (mean * mean)

    down = [(i + 1, i) for i in range(nc - 1)]
    upward = [(i, i + 1) for i in range(nc - 1)]
    outward = [(1, 0), (2, 3)]
    down1 = [lax.ppermute(band0[i], "tcol", down) for i in range(PIECES)]
    up1 = [lax.ppermute(band1[i], "tcol", upward) for i in range(PIECES)]
    first, second, third, down2, up2 = [], [], [], [], []
    for i in range(PIECES):
        first.append(jnp.where(upper, up1[i], down1[i]))
        payload = jnp.where(z == nc - 1, band1[i], down1[i])
        down2.append(lax.ppermute(payload, "tcol", down))
        payload = jnp.where(z == 0, band0[i], up1[i])
        up2.append(lax.ppermute(payload, "tcol", upward))
    for i in range(PIECES):
        second.append(jnp.where(upper, up2[i], down2[i]))
        moved = lax.ppermute(second[i], "tcol", outward)
        third.append(jnp.where(at_end, moved, jnp.where(upper, down2[i], up2[i])))
    stream = own + first + second + third
    blocks = [[0, 1, 2, 3], [1, 2, 3, 0], [2, 1, 0, 3], [3, 2, 1, 0]]
    half = nc // 2
    table = []
    for zz in range(nc):
        for pp in range(npix):
            slots = list(blocks[zz])
            if npix == 2:
                slots = [((b // half) ^ pp) * half + b % half for b in slots]
            line = [b * PIECES + i for b in slots for i in range(PIECES)] + slots
            for k in range(nc):
                line += [blocks[zz if band == zz // half else zz ^ half][k] for band in range(2)]
            table.append(line)
    table = jnp.array(table, jnp.int32)
    same = (t & 2) == (z & 2)
    line = lax.dynamic_slice(table, (z * npix + pix, 0), (1, table.shape[1]))[0]
    flags = jnp.stack([same, upper]).astype(jnp.int32)

    index = lambda a, b: a * nc + b
    across = [
        (index(a, b), index(a ^ 1, b)) for a in range(nt) for b in range(nc) if (a & 1) == (b & 1)
    ]
    swap = [(index(a, b), index(a ^ 2, b)) for a in range(nt) for b in range(nc)]
    source = (t & 1) == (z & 1)
    near, far = [], []
    for k, piece in enumerate(stream):
        got = lax.ppermute(piece, GRID, across)
        near.append(jnp.where(source, piece, got))
        far.append(lax.ppermute(near[-1], GRID, swap))

    staged = None
    for k in range(nc):
        at = slice(k * PIECES, (k + 1) * PIECES)
        scale, *block, _ = lax.optimization_barrier((weight, *stream[at], far[0]))
        staged = stage(staged, line[at], block, scale[None], mean[None], nc * local_frames)
        if k == nc - 2:
            early = staged[0]
    rows, level = staged
    level = level.sum(axis=1)
    count = nc * local_frames // npix
    if npix == 2:
        level = level[:count] + lax.ppermute(level[count:], "pix", [(0, 1), (1, 0)])
    else:
        level = lax.psum_scatter(level, "pix", scatter_dimension=0, tiled=True)
    row_scale = band_pixels / level
    extra = split(1.0 / mean)
    order = line[nc * PIECES : nc * PIECES + nc]
    order = jnp.stack([order, order])
    everything = nc * local_frames
    tile = 256 if count % 256 == 0 else local_frames
    tiles = lambda start, n: jnp.array([range(start, start + n), range(n)], jnp.int32)

    def correlate(cols, gate, ahead):
        other_core = [(0, 1), (1, 0)]
        if npix == 2 and ahead:
            slots = order[:, : nc - 1]
            sums, part = gram(early, local_frames, slots, nc, cols, extra, step=256)
            slots = order[:, nc - 1 :]
            (part,) = gram(rows, local_frames, slots, nc, cols, prev=part, step=384)
            total, theirs = part[:count], lax.ppermute(part[count:], "pix", other_core)
        elif npix == 2:
            n = count // tile
            sums, theirs = gram(rows, tile, tiles(n, n), n, cols, extra)
            theirs = lax.ppermute(theirs, "pix", other_core)
            (total,) = gram(rows, tile, tiles(0, n), n, cols)
        else:
            n = everything // tile
            sums, part = gram(rows, tile, tiles(0, n), n, cols, extra)
            total = lax.psum_scatter(part, "pix", scatter_dimension=0, tiled=True)
            theirs = jnp.zeros_like(total)
        sums = sums[:3].sum(axis=0)
        if npix == 2:
            sums = sums + lax.ppermute(sums, "pix", other_core)
        else:
            sums = lax.psum(sums, "pix")
        theirs, gate = lax.optimization_barrier((theirs, gate))
        return (total + theirs) * row_scale[:, None] * (1.0 / sums)[None, :]

    over = [(i, i ^ 2) for i in range(nc)]
    chunks = [[(k, 0, PIECES)] for k in range(nc - 1)] + [[(nc - 1, i, 1) for i in range(PIECES)]]
    gate, outs, n = row_scale, None, 0
    for parts in chunks:
        values, ships = [], []
        for k, i, size in parts:
            lo = k * PIECES + i
            value = correlate(near[lo : lo + size] + far[lo : lo + size], gate, k == 0)
            a, b = value[:, : size * height], value[:, size * height :]
            gate = (jnp.where(same, b, a) - 1.0).astype(SHIP)
            values.append(value)
            ships.append(lax.ppermute(gate, "tcol", over).astype(jnp.float32) + 1.0)
            n += 1
        at = nc * PIECES + nc + 2 * k
        info = jnp.concatenate([line[at : at + 2], flags])
        outs = place(outs, info, values, ships, nc * local_frames)
    return outs[0], outs[1]


def solution(mesh):
    in_specs = (P(("trow", "tcol"), None, "pix", None), P(("trow", "tcol"), None))
    out_specs = (P(("trow", "pix"), "tcol"), P(("trow", "pix"), "tcol"))

    return jax.shard_map(
        per_device, mesh=mesh, in_specs=in_specs, out_specs=out_specs, check_vma=False
    )
```

```python
import functools

import jax
import jax.numpy as jnp
from jax import lax
from jax.experimental import pallas as pl
from jax.experimental.pallas import tpu as pltpu
from jax.sharding import PartitionSpec as P


PIECES = 2
SHIP = jnp.float16
EXTRA = 16
GRID = ("trow", "tcol")


def edge_kernel(first_ref, last_ref, head_ref, tail_ref):
    f, rows, cols = first_ref.shape[0], first_ref.shape[2], first_ref.shape[3]
    for ref, out, r in ((first_ref, head_ref, 0), (last_ref, tail_ref, rows - 1)):
        flat = ref.reshape(f * rows, cols)
        out[0] = flat[pl.ds(r, f, stride=rows), :].astype(jnp.bfloat16)


def edges(frames):
    n, bands, rows, cols = frames.shape
    group = min(8, rows)
    fb = n // 2
    block = (fb, 1, group, cols)
    out = pl.BlockSpec((1, fb, cols), lambda b, i: (b, i, 0))
    shape = jax.ShapeDtypeStruct((bands, n, cols), jnp.bfloat16)
    return pl.pallas_call(
        edge_kernel,
        grid=(bands, n // fb),
        in_specs=[
            pl.BlockSpec(block, lambda b, i: (i, b, 0, 0)),
            pl.BlockSpec(block, lambda b, i: (i, b, rows // group - 1, 0)),
        ],
        out_specs=[out, out],
        out_shape=[shape, shape],
        name="edges",
    )(frames, frames)


def shift_kernel(beta_ref, x_ref, lo_ref, hi_ref, d_ref, s0_ref, s1_ref, own_ref, sum_ref, cs):
    f, bands, rows, cols = x_ref.shape
    flat = x_ref.reshape(f * bands * rows, cols)
    steps = d_ref[...]

    def share(v):
        return jnp.broadcast_to(v.astype(jnp.float32) * 0.125, (f, cols))

    lane = lax.broadcasted_iota(jnp.int32, (f, cols), 1)
    by_row, by_col = steps[:, 0:1], steps[:, 1:2]
    up, down = share(jnp.maximum(by_row, 0)), share(jnp.maximum(-by_row, 0))
    cs[0], cs[1], cs[2] = 1.0 - up - down, up, down
    up, down = share(jnp.maximum(by_col, 0)), share(jnp.maximum(-by_col, 0))
    cs[3] = 1.0 - up - down
    cs[4] = jnp.where(lane == cols - 1, 0.0, up)
    cs[5] = jnp.where(lane == 0, 0.0, down)

    @pl.when(pl.program_id(0) == 0)
    def _():
        sum_ref[...] = jnp.zeros_like(sum_ref)

    for band, s_ref in ((0, s0_ref), (1, s1_ref)):

        def row(r):
            if r < 0:
                return lo_ref[band].astype(jnp.float32)
            if r >= rows:
                return hi_ref[band].astype(jnp.float32)
            return flat[pl.ds(band * rows + r, f, stride=bands * rows), :]

        before, here = row(-1), row(0)
        for r in range(rows):
            after = row(r + 1)
            p = cs[0] * here + cs[1] * after + cs[2] * before
            s = cs[3] * p + cs[4] * pltpu.roll(p, cols - 1, 1) + cs[5] * pltpu.roll(p, 1, 1)
            s = s.astype(jnp.bfloat16)
            s_ref[:, r * cols : (r + 1) * cols] = s
            part = jnp.sum(s.astype(jnp.float32).reshape(f // 8, 8, cols), axis=0)
            sum_ref[band, r * 8 : r * 8 + 8, :] += part
            before, here = here, after

        @pl.when(beta_ref[0] == band)
        def _():
            own_ref[...] = s_ref[...]


def shift(beta, frames, lo, hi, drift, start, count):
    _, bands, rows, cols = frames.shape
    fb = count
    while fb > 64 and fb % 2 == 0:
        fb //= 2
    first = start // fb
    edge = pl.BlockSpec((bands, fb, cols), lambda i, _: (0, i + first, 0))
    out = pl.BlockSpec((fb, rows * cols), lambda i, _: (i, 0))
    shape = jax.ShapeDtypeStruct((count, rows * cols), jnp.bfloat16)
    return pl.pallas_call(
        shift_kernel,
        grid_spec=pltpu.PrefetchScalarGridSpec(
            num_scalar_prefetch=1,
            grid=(count // fb,),
            in_specs=[
                pl.BlockSpec((fb, bands, rows, cols), lambda i, _: (i + first, 0, 0, 0)),
                edge,
                edge,
                pl.BlockSpec((fb, 2), lambda i, _: (i + first, 0)),
            ],
            out_specs=[
                out,
                out,
                out,
                pl.BlockSpec((bands, rows * 8, cols), lambda i, _: (0, 0, 0)),
            ],
            scratch_shapes=[pltpu.VMEM((6, fb, cols), jnp.float32)],
        ),
        out_shape=[shape, shape, shape, jax.ShapeDtypeStruct((bands, rows * 8, cols), jnp.float32)],
        cost_estimate=pl.CostEstimate(
            flops=count * bands * rows * cols * 12,
            bytes_accessed=count * bands * rows * cols * 7,
            transcendentals=0,
        ),
        name="shift",
    )(beta, frames, lo, hi, drift)


def gram_kernel(extra, step, pieces, slots_ref, *refs):
    refs = list(refs)
    e_ref = refs.pop(0) if extra else None
    a_ref = refs.pop(0)
    c_refs = refs[:pieces]
    o_ref, c_ref = refs[-2:]

    @pl.when(pl.program_id(0) == 0)
    def _():
        at = 0
        for ref in c_refs:
            c_ref[at : at + ref.shape[0], :] = ref[...]
            at += ref.shape[0]

    a = a_ref[...]
    if extra:
        a = jnp.concatenate([e_ref[...], a], axis=0)
    width = o_ref.shape[1]

    def chunk(at):
        part = lax.dot_general(
            a, c_ref[at, :], (((1,), (1,)), ((), ())), preferred_element_type=jnp.float32
        )
        if extra:
            refs[-3][:, at] = part[:EXTRA]
            part = part[EXTRA:]
        o_ref[:, at] = part

    if step < width and width % step == 0:

        @pl.loop(0, width // step)
        def _(j):
            chunk(pl.ds(pl.multiple_of(j * step, step), step))

    else:
        chunk(slice(0, width))


def gram(rows, height, slots, total, pieces, extra=None, prev=None, step=1024):
    depth = rows.shape[1]
    n = slots.shape[1]
    width = sum(p.shape[0] for p in pieces)
    fixed = lambda shape: pl.BlockSpec(shape, lambda i, s: (0, 0), pipeline_mode=pl.Buffered(1))
    in_specs = [pl.BlockSpec((height, depth), lambda i, s: (s[0, i], 0))]
    in_specs += [fixed(p.shape) for p in pieces]
    out_specs = [pl.BlockSpec((height, width), lambda i, s: (s[1, i], 0))]
    out_shape = [jax.ShapeDtypeStruct((total * height, width), jnp.float32)]
    args = [rows, *pieces]
    if extra is not None:
        in_specs.insert(0, fixed((EXTRA, depth)))
        out_specs.insert(0, pl.BlockSpec((EXTRA, width), lambda i, s: (0, 0)))
        out_shape.insert(0, jax.ShapeDtypeStruct((EXTRA, width), jnp.float32))
        args.insert(0, extra)
    aliases = {}
    if prev is not None:
        in_specs.append(pl.BlockSpec(memory_space=pl.ANY))
        aliases = {len(args) + 1: 0}
        args.append(prev)
    return pl.pallas_call(
        functools.partial(gram_kernel, extra is not None, step, len(pieces)),
        grid_spec=pltpu.PrefetchScalarGridSpec(
            num_scalar_prefetch=1,
            grid=(n,),
            in_specs=in_specs,
            out_specs=out_specs,
            scratch_shapes=[pltpu.VMEM((width, depth), jnp.bfloat16)],
        ),
        out_shape=out_shape,
        input_output_aliases=aliases,
        cost_estimate=pl.CostEstimate(
            flops=2 * n * height * width * depth,
            bytes_accessed=2 * depth * (n * height + width) + 4 * n * height * width,
            transcendentals=0,
        ),
        name="gram",
    )(slots, *args)


def halves_kernel(pieces, e_ref, a_ref, *refs):
    c_refs = refs[:pieces]
    x_ref, theirs_ref, mine_ref, c_ref = refs[pieces:]
    step, half = pl.program_id(0), pl.num_programs(0) // 2

    @pl.when(step == 0)
    def _():
        at = 0
        for ref in c_refs:
            c_ref[at : at + ref.shape[0], :] = ref[...]
            at += ref.shape[0]

    def dot(a):
        return lax.dot_general(
            a, c_ref[...], (((1,), (1,)), ((), ())), preferred_element_type=jnp.float32
        )

    @pl.when(step < half)
    def _():
        part = dot(jnp.concatenate([e_ref[...], a_ref[...]], axis=0))
        x_ref[...] = part[:EXTRA]
        theirs_ref[...] = part[EXTRA:]

    @pl.when(step >= half)
    def _():
        mine_ref[...] = dot(a_ref[...])


def gram_halves(rows, pieces, extra):
    total, depth = rows.shape
    half = total // 2
    tile = 256 if half % 256 == 0 else half
    n = half // tile
    width = sum(p.shape[0] for p in pieces)
    fixed = lambda shape: pl.BlockSpec(shape, lambda i: (0, 0), pipeline_mode=pl.Buffered(1))
    shape = jax.ShapeDtypeStruct((half, width), jnp.float32)
    return pl.pallas_call(
        functools.partial(halves_kernel, len(pieces)),
        grid=(2 * n,),
        in_specs=[
            fixed((EXTRA, depth)),
            pl.BlockSpec((tile, depth), lambda i: ((i + n) % (2 * n), 0)),
            *[fixed(p.shape) for p in pieces],
        ],
        out_specs=[
            pl.BlockSpec((EXTRA, width), lambda i: (0, 0)),
            pl.BlockSpec((tile, width), lambda i: (jnp.minimum(i, n - 1), 0)),
            pl.BlockSpec((tile, width), lambda i: (jnp.maximum(i - n, 0), 0)),
        ],
        out_shape=[jax.ShapeDtypeStruct((EXTRA, width), jnp.float32), shape, shape],
        scratch_shapes=[pltpu.VMEM((width, depth), jnp.bfloat16)],
        cost_estimate=pl.CostEstimate(
            flops=2 * total * width * depth,
            bytes_accessed=2 * depth * (total + width) + 4 * total * width,
            transcendentals=0,
        ),
        name="gram_halves",
    )(extra, rows, *pieces)


def stage_kernel(pieces, slots_ref, *refs):
    c_refs, w_ref, m_ref = refs[:pieces], refs[pieces], refs[pieces + 1]
    o_ref, l_ref = refs[-2:]
    lanes = l_ref.shape[1]
    for i in range(pieces):

        @pl.when(pl.program_id(0) == i)
        def _():

            def body(c, level):
                at = pl.ds(pl.multiple_of(c * lanes, lanes), lanes)
                value = c_refs[i][:, at].astype(jnp.float32) * w_ref[:, at]
                value = value.astype(jnp.bfloat16)
                o_ref[:, at] = value
                return level + value.astype(jnp.float32) * m_ref[:, at]

            chunks = o_ref.shape[1] // lanes
            level = lax.fori_loop(0, chunks, body, jnp.zeros(l_ref.shape, jnp.float32))
            l_ref[...] = level


def stage(prev, slots, pieces, weight, mean, total):
    height, depth = pieces[0].shape
    n = len(pieces)
    lanes = min(128, depth)
    fixed = lambda shape: pl.BlockSpec(shape, lambda i, _: (0, 0), pipeline_mode=pl.Buffered(1))
    in_specs = [fixed((height, depth)) for _ in pieces] + [fixed((1, depth))] * 2
    args = [slots, *pieces, weight, mean]
    aliases = {}
    if prev is not None:
        aliases = {len(args): 0, len(args) + 1: 1}
        in_specs += [pl.BlockSpec(memory_space=pl.ANY)] * 2
        args += prev
    return pl.pallas_call(
        functools.partial(stage_kernel, n),
        grid_spec=pltpu.PrefetchScalarGridSpec(
            num_scalar_prefetch=1,
            grid=(n,),
            in_specs=in_specs,
            out_specs=[
                pl.BlockSpec((height, depth), lambda i, s: (s[i], 0)),
                pl.BlockSpec((height, lanes), lambda i, s: (s[i], 0)),
            ],
        ),
        out_shape=[
            jax.ShapeDtypeStruct((total, depth), jnp.bfloat16),
            jax.ShapeDtypeStruct((total, lanes), jnp.float32),
        ],
        input_output_aliases=aliases,
        cost_estimate=pl.CostEstimate(
            flops=n * height * depth, bytes_accessed=4 * n * height * depth, transcendentals=0
        ),
        name="stage",
    )(*args)


def place_kernel(parts, info_ref, *refs):
    values, ships = refs[:parts], refs[parts : 2 * parts]
    first_ref, second_ref = refs[-2:]
    width = ships[0].shape[1]
    same, upper = info_ref[2] == 1, info_ref[3] == 1
    for i in range(parts):
        at = slice(i * width, (i + 1) * width)
        a, b = values[i][:, :width], values[i][:, width:]
        keep = jnp.where(same, a, b)
        ship = ships[i][...]
        first_ref[:, at] = jnp.where(upper, ship, keep)
        second_ref[:, at] = jnp.where(upper, keep, ship)


def place(outs, info, values, ships, total):
    count = values[0].shape[0]
    parts = len(values)
    width = ships[0].shape[1]
    tile = count // 3 if count % 24 == 0 else count
    in_specs = [pl.BlockSpec((tile, 2 * width), lambda i, _: (i, 0))] * parts
    in_specs += [pl.BlockSpec((tile, width), lambda i, _: (i, 0))] * parts
    args = [info, *values, *ships]
    aliases = {}
    if outs is not None:
        aliases = {len(args): 0, len(args) + 1: 1}
        in_specs += [pl.BlockSpec(memory_space=pl.ANY)] * 2
        args += outs
    shape = jax.ShapeDtypeStruct((count, total), jnp.float32)
    return pl.pallas_call(
        functools.partial(place_kernel, parts),
        grid_spec=pltpu.PrefetchScalarGridSpec(
            num_scalar_prefetch=1,
            grid=(count // tile,),
            in_specs=in_specs,
            out_specs=[
                pl.BlockSpec((tile, parts * width), lambda i, s: (i, s[0])),
                pl.BlockSpec((tile, parts * width), lambda i, s: (i, s[1])),
            ],
        ),
        out_shape=[shape, shape],
        input_output_aliases=aliases,
        cost_estimate=pl.CostEstimate(
            flops=4 * count * width * parts,
            bytes_accessed=18 * count * width * parts,
            transcendentals=0,
        ),
        name="place",
    )(*args)


def split(x):
    parts = []
    for _ in range(3):
        part = lax.reduce_precision(x, 8, 7)
        parts.append(part.astype(jnp.bfloat16))
        x = x - part
    pad = jnp.zeros((EXTRA - 3,) + x.shape, jnp.bfloat16)
    return jnp.concatenate([jnp.stack(parts), pad])


def per_device(frames, drift):
    local_frames, _, tile_rows, columns = frames.shape
    nt, nc, npix = (lax.axis_size(a) for a in ("trow", "tcol", "pix"))
    assert nt == 4 and nc == 4
    total_frames = local_frames * nt * nc
    pixels = tile_rows * columns
    band_pixels = pixels * npix
    t, z, pix = (lax.axis_index(a) for a in ("trow", "tcol", "pix"))
    upper = z >= 2
    at_end = (z == 0) | (z == nc - 1)
    beta = upper.astype(jnp.int32)
    height = local_frames // PIECES

    head, tail = edges(frames)
    lo = lax.ppermute(tail, "pix", [(i, i + 1) for i in range(npix - 1)])
    hi = lax.ppermute(head, "pix", [(i + 1, i) for i in range(npix - 1)])
    parts = [shift(beta[None], frames, lo, hi, drift, i * height, height) for i in range(PIECES)]
    band0, band1, own, sums = ([part[j] for part in parts] for j in range(4))

    total = sum(sums).reshape(2, tile_rows, 8, columns).sum(axis=2)
    for axis, step in (("trow", 1), ("trow", 2), ("tcol", 1), ("tcol", 2)):
        total = total + lax.ppermute(total, axis, [(i, i ^ step) for i in range(4)])
    mean = (jnp.where(upper, total[1], total[0]) / total_frames).reshape(pixels)
    weight = 1.0 / (mean * mean)

    down = [(i + 1, i) for i in range(nc - 1)]
    upward = [(i, i + 1) for i in range(nc - 1)]
    outward = [(1, 0), (2, 3)]
    down1 = [lax.ppermute(band0[i], "tcol", down) for i in range(PIECES)]
    up1 = [lax.ppermute(band1[i], "tcol", upward) for i in range(PIECES)]
    first, second, third, down2, up2 = [], [], [], [], []
    for i in range(PIECES):
        first.append(jnp.where(upper, up1[i], down1[i]))
        payload = jnp.where(z == nc - 1, band1[i], down1[i])
        down2.append(lax.ppermute(payload, "tcol", down))
        payload = jnp.where(z == 0, band0[i], up1[i])
        up2.append(lax.ppermute(payload, "tcol", upward))
    for i in range(PIECES):
        second.append(jnp.where(upper, up2[i], down2[i]))
        moved = lax.ppermute(second[i], "tcol", outward)
        third.append(jnp.where(at_end, moved, jnp.where(upper, down2[i], up2[i])))
    stream = own + first + second + third
    blocks = [[0, 1, 2, 3], [1, 2, 3, 0], [2, 1, 0, 3], [3, 2, 1, 0]]
    half = nc // 2
    table = []
    for zz in range(nc):
        for pp in range(npix):
            slots = list(blocks[zz])
            if npix == 2:
                slots = [((b // half) ^ pp) * half + b % half for b in slots]
            line = [b * PIECES + i for b in slots for i in range(PIECES)] + slots
            for k in range(nc):
                line += [blocks[zz if band == zz // half else zz ^ half][k] for band in range(2)]
            table.append(line)
    table = jnp.array(table, jnp.int32)
    same = (t & 2) == (z & 2)
    line = lax.dynamic_slice(table, (z * npix + pix, 0), (1, table.shape[1]))[0]
    flags = jnp.stack([same, upper]).astype(jnp.int32)

    index = lambda a, b: a * nc + b
    across = [
        (index(a, b), index(a ^ 1, b)) for a in range(nt) for b in range(nc) if (a & 1) == (b & 1)
    ]
    swap = [(index(a, b), index(a ^ 2, b)) for a in range(nt) for b in range(nc)]
    source = (t & 1) == (z & 1)
    near, far = [], []
    for k, piece in enumerate(stream):
        got = lax.ppermute(piece, GRID, across)
        near.append(jnp.where(source, piece, got))
        far.append(lax.ppermute(near[-1], GRID, swap))

    staged = None
    for k in range(nc):
        at = slice(k * PIECES, (k + 1) * PIECES)
        scale, *block, _ = lax.optimization_barrier((weight, *stream[at], far[0]))
        staged = stage(staged, line[at], block, scale[None], mean[None], nc * local_frames)
        if k == nc - 2:
            early = staged[0]
    rows, level = staged
    level = level.sum(axis=1)
    count = nc * local_frames // npix
    if npix == 2:
        level = level[:count] + lax.ppermute(level[count:], "pix", [(0, 1), (1, 0)])
    else:
        level = lax.psum_scatter(level, "pix", scatter_dimension=0, tiled=True)
    row_scale = band_pixels / level
    extra = split(1.0 / mean)
    order = line[nc * PIECES : nc * PIECES + nc]
    order = jnp.stack([order, order])
    everything = nc * local_frames
    tile = 256 if count % 256 == 0 else local_frames
    tiles = lambda start, n: jnp.array([range(start, start + n), range(n)], jnp.int32)

    def correlate(cols, gate, ahead):
        other_core = [(0, 1), (1, 0)]
        if npix == 2 and ahead:
            slots = order[:, : nc - 1]
            sums, part = gram(early, local_frames, slots, nc, cols, extra, step=256)
            slots = order[:, nc - 1 :]
            (part,) = gram(rows, local_frames, slots, nc, cols, prev=part, step=384)
            total, theirs = part[:count], lax.ppermute(part[count:], "pix", other_core)
        elif npix == 2:
            sums, theirs, total = gram_halves(rows, cols, extra)
            theirs = lax.ppermute(theirs, "pix", other_core)
        else:
            n = everything // tile
            sums, part = gram(rows, tile, tiles(0, n), n, cols, extra)
            total = lax.psum_scatter(part, "pix", scatter_dimension=0, tiled=True)
            theirs = jnp.zeros_like(total)
        sums = sums[:3].sum(axis=0)
        if npix == 2:
            sums = sums + lax.ppermute(sums, "pix", other_core)
        else:
            sums = lax.psum(sums, "pix")
        theirs, gate = lax.optimization_barrier((theirs, gate))
        return (total + theirs) * row_scale[:, None] * (1.0 / sums)[None, :]

    over = [(i, i ^ 2) for i in range(nc)]
    chunks = [[(k, 0, PIECES)] for k in range(nc - 1)] + [[(nc - 1, i, 1) for i in range(PIECES)]]
    gate, outs, n = row_scale, None, 0
    for parts in chunks:
        values, ships = [], []
        for k, i, size in parts:
            lo = k * PIECES + i
            value = correlate(near[lo : lo + size] + far[lo : lo + size], gate, k < 2)
            a, b = value[:, : size * height], value[:, size * height :]
            gate = (jnp.where(same, b, a) - 1.0).astype(SHIP)
            values.append(value)
            ships.append(lax.ppermute(gate, "tcol", over).astype(jnp.float32) + 1.0)
            n += 1
        at = nc * PIECES + nc + 2 * k
        info = jnp.concatenate([line[at : at + 2], flags])
        outs = place(outs, info, values, ships, nc * local_frames)
    return outs[0], outs[1]


def solution(mesh):
    in_specs = (P(("trow", "tcol"), None, "pix", None), P(("trow", "tcol"), None))
    out_specs = (P(("trow", "pix"), "tcol"), P(("trow", "pix"), "tcol"))

    return jax.shard_map(
        per_device, mesh=mesh, in_specs=in_specs, out_specs=out_specs, check_vma=False
    )
```

```python
import functools

import jax
import jax.numpy as jnp
from jax import lax
from jax.experimental import pallas as pl
from jax.experimental.pallas import tpu as pltpu
from jax.sharding import PartitionSpec as P


PIECES = 2
SHIP = jnp.float16
EXTRA = 16
GRID = ("trow", "tcol")


def edge_kernel(first_ref, last_ref, head_ref, tail_ref):
    f, rows, cols = first_ref.shape[0], first_ref.shape[2], first_ref.shape[3]
    for ref, out, r in ((first_ref, head_ref, 0), (last_ref, tail_ref, rows - 1)):
        flat = ref.reshape(f * rows, cols)
        out[0] = flat[pl.ds(r, f, stride=rows), :].astype(jnp.bfloat16)


def edges(frames):
    n, bands, rows, cols = frames.shape
    group = min(8, rows)
    fb = n // 2
    block = (fb, 1, group, cols)
    out = pl.BlockSpec((1, fb, cols), lambda b, i: (b, i, 0))
    shape = jax.ShapeDtypeStruct((bands, n, cols), jnp.bfloat16)
    return pl.pallas_call(
        edge_kernel,
        grid=(bands, n // fb),
        in_specs=[
            pl.BlockSpec(block, lambda b, i: (i, b, 0, 0)),
            pl.BlockSpec(block, lambda b, i: (i, b, rows // group - 1, 0)),
        ],
        out_specs=[out, out],
        out_shape=[shape, shape],
        name="edges",
    )(frames, frames)


def shift_kernel(beta_ref, x_ref, lo_ref, hi_ref, d_ref, s0_ref, s1_ref, own_ref, sum_ref):
    frames, bands, rows, cols = x_ref.shape
    f = 16 if frames % 16 == 0 else frames
    flat = x_ref.reshape(frames * bands * rows, cols)

    @pl.when(pl.program_id(0) == 0)
    def _():
        sum_ref[...] = jnp.zeros_like(sum_ref)

    @pl.loop(0, frames // f)
    def _(g):
        base = pl.multiple_of(g * f, f)
        group = pl.ds(base, f)
        steps = d_ref[group, :]

        def share(v):
            return jnp.broadcast_to(v.astype(jnp.float32) * 0.125, (f, cols))

        lane = lax.broadcasted_iota(jnp.int32, (f, cols), 1)
        by_row, by_col = steps[:, 0:1], steps[:, 1:2]
        up, down = share(jnp.maximum(by_row, 0)), share(jnp.maximum(-by_row, 0))
        stay = 1.0 - up - down
        right, left = share(jnp.maximum(by_col, 0)), share(jnp.maximum(-by_col, 0))
        keep = 1.0 - right - left
        right = jnp.where(lane == cols - 1, 0.0, right)
        left = jnp.where(lane == 0, 0.0, left)

        for band, s_ref in ((0, s0_ref), (1, s1_ref)):

            def row(r):
                if r < 0:
                    return lo_ref[band, group, :].astype(jnp.float32)
                if r >= rows:
                    return hi_ref[band, group, :].astype(jnp.float32)
                start = base * (bands * rows) + (band * rows + r)
                return flat[pl.ds(start, f, stride=bands * rows), :]

            before, here = row(-1), row(0)
            for r in range(rows):
                after = row(r + 1)
                p = stay * here + up * after + down * before
                s = keep * p + right * pltpu.roll(p, cols - 1, 1) + left * pltpu.roll(p, 1, 1)
                s = s.astype(jnp.bfloat16)
                s_ref[group, r * cols : (r + 1) * cols] = s
                part = jnp.sum(s.astype(jnp.float32).reshape(f // 8, 8, cols), axis=0)
                sum_ref[band, r * 8 : r * 8 + 8, :] += part
                before, here = here, after

    for band, s_ref in ((0, s0_ref), (1, s1_ref)):

        @pl.when(beta_ref[0] == band)
        def _():
            own_ref[...] = s_ref[...]


def shift(beta, frames, lo, hi, drift, start, count):
    _, bands, rows, cols = frames.shape
    fb = count
    while fb > 64 and fb % 2 == 0:
        fb //= 2
    first = start // fb
    edge = pl.BlockSpec((bands, fb, cols), lambda i, _: (0, i + first, 0))
    out = pl.BlockSpec((fb, rows * cols), lambda i, _: (i, 0))
    shape = jax.ShapeDtypeStruct((count, rows * cols), jnp.bfloat16)
    return pl.pallas_call(
        shift_kernel,
        grid_spec=pltpu.PrefetchScalarGridSpec(
            num_scalar_prefetch=1,
            grid=(count // fb,),
            in_specs=[
                pl.BlockSpec((fb, bands, rows, cols), lambda i, _: (i + first, 0, 0, 0)),
                edge,
                edge,
                pl.BlockSpec((fb, 2), lambda i, _: (i + first, 0)),
            ],
            out_specs=[
                out,
                out,
                out,
                pl.BlockSpec((bands, rows * 8, cols), lambda i, _: (0, 0, 0)),
            ],
        ),
        out_shape=[shape, shape, shape, jax.ShapeDtypeStruct((bands, rows * 8, cols), jnp.float32)],
        cost_estimate=pl.CostEstimate(
            flops=count * bands * rows * cols * 12,
            bytes_accessed=count * bands * rows * cols * 7,
            transcendentals=0,
        ),
        name="shift",
    )(beta, frames, lo, hi, drift)


def gram_kernel(extra, step, pieces, slots_ref, *refs):
    refs = list(refs)
    e_ref = refs.pop(0) if extra else None
    a_ref = refs.pop(0)
    c_refs = refs[:pieces]
    o_ref, c_ref = refs[-2:]

    @pl.when(pl.program_id(0) == 0)
    def _():
        at = 0
        for ref in c_refs:
            c_ref[at : at + ref.shape[0], :] = ref[...]
            at += ref.shape[0]

    a = a_ref[...]
    if extra:
        a = jnp.concatenate([e_ref[...], a], axis=0)
    width = o_ref.shape[1]

    def chunk(at):
        part = lax.dot_general(
            a, c_ref[at, :], (((1,), (1,)), ((), ())), preferred_element_type=jnp.float32
        )
        if extra:
            refs[-3][:, at] = part[:EXTRA]
            part = part[EXTRA:]
        o_ref[:, at] = part

    if step < width and width % step == 0:

        @pl.loop(0, width // step)
        def _(j):
            chunk(pl.ds(pl.multiple_of(j * step, step), step))

    else:
        chunk(slice(0, width))


def gram(rows, height, slots, total, pieces, extra=None, prev=None, step=1024):
    depth = rows.shape[1]
    n = slots.shape[1]
    width = sum(p.shape[0] for p in pieces)
    fixed = lambda shape: pl.BlockSpec(shape, lambda i, s: (0, 0), pipeline_mode=pl.Buffered(1))
    in_specs = [pl.BlockSpec((height, depth), lambda i, s: (s[0, i], 0))]
    in_specs += [fixed(p.shape) for p in pieces]
    out_specs = [pl.BlockSpec((height, width), lambda i, s: (s[1, i], 0))]
    out_shape = [jax.ShapeDtypeStruct((total * height, width), jnp.float32)]
    args = [rows, *pieces]
    if extra is not None:
        in_specs.insert(0, fixed((EXTRA, depth)))
        out_specs.insert(0, pl.BlockSpec((EXTRA, width), lambda i, s: (0, 0)))
        out_shape.insert(0, jax.ShapeDtypeStruct((EXTRA, width), jnp.float32))
        args.insert(0, extra)
    aliases = {}
    if prev is not None:
        in_specs.append(pl.BlockSpec(memory_space=pl.ANY))
        aliases = {len(args) + 1: 0}
        args.append(prev)
    return pl.pallas_call(
        functools.partial(gram_kernel, extra is not None, step, len(pieces)),
        grid_spec=pltpu.PrefetchScalarGridSpec(
            num_scalar_prefetch=1,
            grid=(n,),
            in_specs=in_specs,
            out_specs=out_specs,
            scratch_shapes=[pltpu.VMEM((width, depth), jnp.bfloat16)],
        ),
        out_shape=out_shape,
        input_output_aliases=aliases,
        cost_estimate=pl.CostEstimate(
            flops=2 * n * height * width * depth,
            bytes_accessed=2 * depth * (n * height + width) + 4 * n * height * width,
            transcendentals=0,
        ),
        name="gram",
    )(slots, *args)


def halves_kernel(pieces, e_ref, a_ref, *refs):
    c_refs = refs[:pieces]
    x_ref, theirs_ref, mine_ref, c_ref = refs[pieces:]
    step, half = pl.program_id(0), pl.num_programs(0) // 2

    @pl.when(step == 0)
    def _():
        at = 0
        for ref in c_refs:
            c_ref[at : at + ref.shape[0], :] = ref[...]
            at += ref.shape[0]

    def dot(a):
        return lax.dot_general(
            a, c_ref[...], (((1,), (1,)), ((), ())), preferred_element_type=jnp.float32
        )

    @pl.when(step < half)
    def _():
        part = dot(jnp.concatenate([e_ref[...], a_ref[...]], axis=0))
        x_ref[...] = part[:EXTRA]
        theirs_ref[...] = part[EXTRA:]

    @pl.when(step >= half)
    def _():
        mine_ref[...] = dot(a_ref[...])


def gram_halves(rows, pieces, extra):
    total, depth = rows.shape
    half = total // 2
    tile = 256 if half % 256 == 0 else half
    n = half // tile
    width = sum(p.shape[0] for p in pieces)
    fixed = lambda shape: pl.BlockSpec(shape, lambda i: (0, 0), pipeline_mode=pl.Buffered(1))
    shape = jax.ShapeDtypeStruct((half, width), jnp.float32)
    return pl.pallas_call(
        functools.partial(halves_kernel, len(pieces)),
        grid=(2 * n,),
        in_specs=[
            fixed((EXTRA, depth)),
            pl.BlockSpec((tile, depth), lambda i: ((i + n) % (2 * n), 0)),
            *[fixed(p.shape) for p in pieces],
        ],
        out_specs=[
            pl.BlockSpec((EXTRA, width), lambda i: (0, 0)),
            pl.BlockSpec((tile, width), lambda i: (jnp.minimum(i, n - 1), 0)),
            pl.BlockSpec((tile, width), lambda i: (jnp.maximum(i - n, 0), 0)),
        ],
        out_shape=[jax.ShapeDtypeStruct((EXTRA, width), jnp.float32), shape, shape],
        scratch_shapes=[pltpu.VMEM((width, depth), jnp.bfloat16)],
        cost_estimate=pl.CostEstimate(
            flops=2 * total * width * depth,
            bytes_accessed=2 * depth * (total + width) + 4 * total * width,
            transcendentals=0,
        ),
        name="gram_halves",
    )(extra, rows, *pieces)


def stage_kernel(pieces, slots_ref, *refs):
    c_refs, w_ref, m_ref = refs[:pieces], refs[pieces], refs[pieces + 1]
    o_ref, l_ref = refs[-2:]
    lanes = l_ref.shape[1]
    for i in range(pieces):

        @pl.when(pl.program_id(0) == i)
        def _():

            def body(c, level):
                at = pl.ds(pl.multiple_of(c * lanes, lanes), lanes)
                value = c_refs[i][:, at].astype(jnp.float32) * w_ref[:, at]
                value = value.astype(jnp.bfloat16)
                o_ref[:, at] = value
                return level + value.astype(jnp.float32) * m_ref[:, at]

            chunks = o_ref.shape[1] // lanes
            level = lax.fori_loop(0, chunks, body, jnp.zeros(l_ref.shape, jnp.float32))
            l_ref[...] = level


def stage(prev, slots, pieces, weight, mean, total):
    height, depth = pieces[0].shape
    n = len(pieces)
    lanes = min(128, depth)
    fixed = lambda shape: pl.BlockSpec(shape, lambda i, _: (0, 0), pipeline_mode=pl.Buffered(1))
    in_specs = [fixed((height, depth)) for _ in pieces] + [fixed((1, depth))] * 2
    args = [slots, *pieces, weight, mean]
    aliases = {}
    if prev is not None:
        aliases = {len(args): 0, len(args) + 1: 1}
        in_specs += [pl.BlockSpec(memory_space=pl.ANY)] * 2
        args += prev
    return pl.pallas_call(
        functools.partial(stage_kernel, n),
        grid_spec=pltpu.PrefetchScalarGridSpec(
            num_scalar_prefetch=1,
            grid=(n,),
            in_specs=in_specs,
            out_specs=[
                pl.BlockSpec((height, depth), lambda i, s: (s[i], 0)),
                pl.BlockSpec((height, lanes), lambda i, s: (s[i], 0)),
            ],
        ),
        out_shape=[
            jax.ShapeDtypeStruct((total, depth), jnp.bfloat16),
            jax.ShapeDtypeStruct((total, lanes), jnp.float32),
        ],
        input_output_aliases=aliases,
        cost_estimate=pl.CostEstimate(
            flops=n * height * depth, bytes_accessed=4 * n * height * depth, transcendentals=0
        ),
        name="stage",
    )(*args)


def place_kernel(parts, info_ref, *refs):
    values, ships = refs[:parts], refs[parts : 2 * parts]
    first_ref, second_ref = refs[-2:]
    width = ships[0].shape[1]
    same, upper = info_ref[2] == 1, info_ref[3] == 1
    for i in range(parts):
        at = slice(i * width, (i + 1) * width)
        a, b = values[i][:, :width], values[i][:, width:]
        keep = jnp.where(same, a, b)
        ship = ships[i][...]
        first_ref[:, at] = jnp.where(upper, ship, keep)
        second_ref[:, at] = jnp.where(upper, keep, ship)


def place(outs, info, values, ships, total):
    count = values[0].shape[0]
    parts = len(values)
    width = ships[0].shape[1]
    tile = count // 3 if count % 24 == 0 else count
    in_specs = [pl.BlockSpec((tile, 2 * width), lambda i, _: (i, 0))] * parts
    in_specs += [pl.BlockSpec((tile, width), lambda i, _: (i, 0))] * parts
    args = [info, *values, *ships]
    aliases = {}
    if outs is not None:
        aliases = {len(args): 0, len(args) + 1: 1}
        in_specs += [pl.BlockSpec(memory_space=pl.ANY)] * 2
        args += outs
    shape = jax.ShapeDtypeStruct((count, total), jnp.float32)
    return pl.pallas_call(
        functools.partial(place_kernel, parts),
        grid_spec=pltpu.PrefetchScalarGridSpec(
            num_scalar_prefetch=1,
            grid=(count // tile,),
            in_specs=in_specs,
            out_specs=[
                pl.BlockSpec((tile, parts * width), lambda i, s: (i, s[0])),
                pl.BlockSpec((tile, parts * width), lambda i, s: (i, s[1])),
            ],
        ),
        out_shape=[shape, shape],
        input_output_aliases=aliases,
        cost_estimate=pl.CostEstimate(
            flops=4 * count * width * parts,
            bytes_accessed=18 * count * width * parts,
            transcendentals=0,
        ),
        name="place",
    )(*args)


def split(x):
    parts = []
    for _ in range(3):
        part = lax.reduce_precision(x, 8, 7)
        parts.append(part.astype(jnp.bfloat16))
        x = x - part
    pad = jnp.zeros((EXTRA - 3,) + x.shape, jnp.bfloat16)
    return jnp.concatenate([jnp.stack(parts), pad])


def per_device(frames, drift):
    local_frames, _, tile_rows, columns = frames.shape
    nt, nc, npix = (lax.axis_size(a) for a in ("trow", "tcol", "pix"))
    assert nt == 4 and nc == 4
    total_frames = local_frames * nt * nc
    pixels = tile_rows * columns
    band_pixels = pixels * npix
    t, z, pix = (lax.axis_index(a) for a in ("trow", "tcol", "pix"))
    upper = z >= 2
    at_end = (z == 0) | (z == nc - 1)
    beta = upper.astype(jnp.int32)
    height = local_frames // PIECES

    head, tail = edges(frames)
    lo = lax.ppermute(tail, "pix", [(i, i + 1) for i in range(npix - 1)])
    hi = lax.ppermute(head, "pix", [(i + 1, i) for i in range(npix - 1)])
    parts = [shift(beta[None], frames, lo, hi, drift, i * height, height) for i in range(PIECES)]
    band0, band1, own, sums = ([part[j] for part in parts] for j in range(4))

    total = sum(sums).reshape(2, tile_rows, 8, columns).sum(axis=2)
    for axis, step in (("trow", 1), ("trow", 2), ("tcol", 1), ("tcol", 2)):
        total = total + lax.ppermute(total, axis, [(i, i ^ step) for i in range(4)])
    mean = (jnp.where(upper, total[1], total[0]) / total_frames).reshape(pixels)
    weight = 1.0 / (mean * mean)

    down = [(i + 1, i) for i in range(nc - 1)]
    upward = [(i, i + 1) for i in range(nc - 1)]
    outward = [(1, 0), (2, 3)]
    down1 = [lax.ppermute(band0[i], "tcol", down) for i in range(PIECES)]
    up1 = [lax.ppermute(band1[i], "tcol", upward) for i in range(PIECES)]
    first, second, third, down2, up2 = [], [], [], [], []
    for i in range(PIECES):
        first.append(jnp.where(upper, up1[i], down1[i]))
        payload = jnp.where(z == nc - 1, band1[i], down1[i])
        down2.append(lax.ppermute(payload, "tcol", down))
        payload = jnp.where(z == 0, band0[i], up1[i])
        up2.append(lax.ppermute(payload, "tcol", upward))
    for i in range(PIECES):
        second.append(jnp.where(upper, up2[i], down2[i]))
        moved = lax.ppermute(second[i], "tcol", outward)
        third.append(jnp.where(at_end, moved, jnp.where(upper, down2[i], up2[i])))
    stream = own + first + second + third
    blocks = [[0, 1, 2, 3], [1, 2, 3, 0], [2, 1, 0, 3], [3, 2, 1, 0]]
    half = nc // 2
    table = []
    for zz in range(nc):
        for pp in range(npix):
            slots = list(blocks[zz])
            if npix == 2:
                slots = [((b // half) ^ pp) * half + b % half for b in slots]
            line = [b * PIECES + i for b in slots for i in range(PIECES)] + slots
            for k in range(nc):
                line += [blocks[zz if band == zz // half else zz ^ half][k] for band in range(2)]
            table.append(line)
    table = jnp.array(table, jnp.int32)
    same = (t & 2) == (z & 2)
    line = lax.dynamic_slice(table, (z * npix + pix, 0), (1, table.shape[1]))[0]
    flags = jnp.stack([same, upper]).astype(jnp.int32)

    index = lambda a, b: a * nc + b
    across = [
        (index(a, b), index(a ^ 1, b)) for a in range(nt) for b in range(nc) if (a & 1) == (b & 1)
    ]
    swap = [(index(a, b), index(a ^ 2, b)) for a in range(nt) for b in range(nc)]
    source = (t & 1) == (z & 1)
    near, far = [], []
    for k, piece in enumerate(stream):
        got = lax.ppermute(piece, GRID, across)
        near.append(jnp.where(source, piece, got))
        far.append(lax.ppermute(near[-1], GRID, swap))

    staged = None
    for k in range(nc):
        at = slice(k * PIECES, (k + 1) * PIECES)
        scale, *block, _ = lax.optimization_barrier((weight, *stream[at], far[0]))
        staged = stage(staged, line[at], block, scale[None], mean[None], nc * local_frames)
        if k == nc - 2:
            early = staged[0]
    rows, level = staged
    level = level.sum(axis=1)
    count = nc * local_frames // npix
    if npix == 2:
        level = level[:count] + lax.ppermute(level[count:], "pix", [(0, 1), (1, 0)])
    else:
        level = lax.psum_scatter(level, "pix", scatter_dimension=0, tiled=True)
    row_scale = band_pixels / level
    extra = split(1.0 / mean)
    order = line[nc * PIECES : nc * PIECES + nc]
    order = jnp.stack([order, order])
    everything = nc * local_frames
    tile = 256 if count % 256 == 0 else local_frames
    tiles = lambda start, n: jnp.array([range(start, start + n), range(n)], jnp.int32)

    def correlate(name, cols, gate, ahead):
        other_core = [(0, 1), (1, 0)]
        if npix == 2 and ahead:
            slots = order[:, : nc - 1]
            sums, part = gram(early, local_frames, slots, nc, cols, extra, step=256)
            slots = order[:, nc - 1 :]
            (part,) = gram(rows, local_frames, slots, nc, cols, prev=part, step=384)
            total, theirs = part[:count], lax.ppermute(part[count:], "pix", other_core)
        elif npix == 2 and name == 2:
            n = count // tile
            sums, theirs = gram(rows, tile, tiles(n, n), n, cols, extra)
            theirs = lax.ppermute(theirs, "pix", other_core)
            (total,) = gram(rows, tile, tiles(0, n), n, cols)
        elif npix == 2:
            sums, theirs, total = gram_halves(rows, cols, extra)
            theirs = lax.ppermute(theirs, "pix", other_core)
        else:
            n = everything // tile
            sums, part = gram(rows, tile, tiles(0, n), n, cols, extra)
            total = lax.psum_scatter(part, "pix", scatter_dimension=0, tiled=True)
            theirs = jnp.zeros_like(total)
        sums = sums[:3].sum(axis=0)
        if npix == 2:
            sums = sums + lax.ppermute(sums, "pix", other_core)
        else:
            sums = lax.psum(sums, "pix")
        theirs, gate = lax.optimization_barrier((theirs, gate))
        return (total + theirs) * row_scale[:, None] * (1.0 / sums)[None, :]

    over = [(i, i ^ 2) for i in range(nc)]
    chunks = [[(k, 0, PIECES)] for k in range(nc - 1)] + [[(nc - 1, i, 1) for i in range(PIECES)]]
    gate, outs, n = row_scale, None, 0
    for parts in chunks:
        values, ships = [], []
        for k, i, size in parts:
            lo = k * PIECES + i
            value = correlate(n, near[lo : lo + size] + far[lo : lo + size], gate, k < 2)
            a, b = value[:, : size * height], value[:, size * height :]
            gate = (jnp.where(same, b, a) - 1.0).astype(SHIP)
            values.append(value)
            ships.append(lax.ppermute(gate, "tcol", over).astype(jnp.float32) + 1.0)
            n += 1
        at = nc * PIECES + nc + 2 * k
        info = jnp.concatenate([line[at : at + 2], flags])
        outs = place(outs, info, values, ships, nc * local_frames)
    return outs[0], outs[1]


def solution(mesh):
    in_specs = (P(("trow", "tcol"), None, "pix", None), P(("trow", "tcol"), None))
    out_specs = (P(("trow", "pix"), "tcol"), P(("trow", "pix"), "tcol"))

    return jax.shard_map(
        per_device, mesh=mesh, in_specs=in_specs, out_specs=out_specs, check_vma=False
    )
```

```python
import functools

import jax
import jax.numpy as jnp
from jax import lax
from jax.experimental import pallas as pl
from jax.experimental.pallas import tpu as pltpu
from jax.sharding import PartitionSpec as P


PIECES = 2
SHIP = jnp.float16
EXTRA = 16
GRID = ("trow", "tcol")


def edge_kernel(parts, *refs):
    head_ref, tail_ref = refs[-2:]
    for n, ref in enumerate(refs[:-2]):
        f, _, rows, cols = ref.shape
        band, rest = divmod(n, 2 * parts)
        part, last = divmod(rest, 2)
        flat = ref.reshape(f * rows, cols)
        value = flat[pl.ds(rows - 1 if last else 0, f, stride=rows), :].astype(jnp.bfloat16)
        (tail_ref if last else head_ref)[band, part * f : (part + 1) * f, :] = value


def edges(frames):
    n, bands, rows, cols = frames.shape
    group = min(8, rows)
    parts = 2
    specs = []
    for band in range(bands):
        for part in range(parts):
            for block in (0, rows // group - 1):
                at = (part, band, block, 0)
                specs.append(pl.BlockSpec((n // parts, 1, group, cols), lambda i, at=at: at))
    out = pl.BlockSpec((bands, n, cols), lambda i: (0, 0, 0))
    shape = jax.ShapeDtypeStruct((bands, n, cols), jnp.bfloat16)
    return pl.pallas_call(
        functools.partial(edge_kernel, parts),
        grid=(1,),
        in_specs=specs,
        out_specs=[out, out],
        out_shape=[shape, shape],
        name="edges",
    )(*[frames] * len(specs))


def shift_kernel(beta_ref, x_ref, lo_ref, hi_ref, d_ref, s0_ref, s1_ref, own_ref, sum_ref):
    frames, bands, rows, cols = x_ref.shape
    f = 16 if frames % 16 == 0 else frames
    flat = x_ref.reshape(frames * bands * rows, cols)

    @pl.when(pl.program_id(0) == 0)
    def _():
        sum_ref[...] = jnp.zeros_like(sum_ref)

    @pl.loop(0, frames // f)
    def _(g):
        base = pl.multiple_of(g * f, f)
        group = pl.ds(base, f)
        steps = d_ref[group, :]

        def share(v):
            return jnp.broadcast_to(v.astype(jnp.float32) * 0.125, (f, cols))

        lane = lax.broadcasted_iota(jnp.int32, (f, cols), 1)
        by_row, by_col = steps[:, 0:1], steps[:, 1:2]
        up, down = share(jnp.maximum(by_row, 0)), share(jnp.maximum(-by_row, 0))
        stay = 1.0 - up - down
        right, left = share(jnp.maximum(by_col, 0)), share(jnp.maximum(-by_col, 0))
        keep = 1.0 - right - left
        right = jnp.where(lane == cols - 1, 0.0, right)
        left = jnp.where(lane == 0, 0.0, left)

        for band, s_ref in ((0, s0_ref), (1, s1_ref)):

            def row(r):
                if r < 0:
                    return lo_ref[band, group, :].astype(jnp.float32)
                if r >= rows:
                    return hi_ref[band, group, :].astype(jnp.float32)
                start = base * (bands * rows) + (band * rows + r)
                return flat[pl.ds(start, f, stride=bands * rows), :]

            before, here = row(-1), row(0)
            for r in range(rows):
                after = row(r + 1)
                p = stay * here + up * after + down * before
                s = keep * p + right * pltpu.roll(p, cols - 1, 1) + left * pltpu.roll(p, 1, 1)
                s = s.astype(jnp.bfloat16)
                s_ref[group, r * cols : (r + 1) * cols] = s
                part = jnp.sum(s.astype(jnp.float32).reshape(f // 8, 8, cols), axis=0)
                sum_ref[band, r * 8 : r * 8 + 8, :] += part
                before, here = here, after

    for band, s_ref in ((0, s0_ref), (1, s1_ref)):

        @pl.when(beta_ref[0] == band)
        def _():
            own_ref[...] = s_ref[...]


def shift(beta, frames, lo, hi, drift, start, count):
    _, bands, rows, cols = frames.shape
    fb = count
    while fb > 64 and fb % 2 == 0:
        fb //= 2
    first = start // fb
    edge = pl.BlockSpec((bands, fb, cols), lambda i, _: (0, i + first, 0))
    out = pl.BlockSpec((fb, rows * cols), lambda i, _: (i, 0))
    shape = jax.ShapeDtypeStruct((count, rows * cols), jnp.bfloat16)
    return pl.pallas_call(
        shift_kernel,
        grid_spec=pltpu.PrefetchScalarGridSpec(
            num_scalar_prefetch=1,
            grid=(count // fb,),
            in_specs=[
                pl.BlockSpec((fb, bands, rows, cols), lambda i, _: (i + first, 0, 0, 0)),
                edge,
                edge,
                pl.BlockSpec((fb, 2), lambda i, _: (i + first, 0)),
            ],
            out_specs=[
                out,
                out,
                out,
                pl.BlockSpec((bands, rows * 8, cols), lambda i, _: (0, 0, 0)),
            ],
        ),
        out_shape=[shape, shape, shape, jax.ShapeDtypeStruct((bands, rows * 8, cols), jnp.float32)],
        cost_estimate=pl.CostEstimate(
            flops=count * bands * rows * cols * 12,
            bytes_accessed=count * bands * rows * cols * 7,
            transcendentals=0,
        ),
        name="shift",
    )(beta, frames, lo, hi, drift)


def gram_kernel(extra, step, pieces, slots_ref, *refs):
    refs = list(refs)
    e_ref = refs.pop(0) if extra else None
    a_ref = refs.pop(0)
    c_refs = refs[:pieces]
    o_ref, c_ref = refs[-2:]

    @pl.when(pl.program_id(0) == 0)
    def _():
        at = 0
        for ref in c_refs:
            c_ref[at : at + ref.shape[0], :] = ref[...]
            at += ref.shape[0]

    a = a_ref[...]
    if extra:
        a = jnp.concatenate([e_ref[...], a], axis=0)
    width = o_ref.shape[1]

    def chunk(at):
        part = lax.dot_general(
            a, c_ref[at, :], (((1,), (1,)), ((), ())), preferred_element_type=jnp.float32
        )
        if extra:
            refs[-3][:, at] = part[:EXTRA]
            part = part[EXTRA:]
        o_ref[:, at] = part

    if step < width and width % step == 0:

        @pl.loop(0, width // step)
        def _(j):
            chunk(pl.ds(pl.multiple_of(j * step, step), step))

    else:
        chunk(slice(0, width))


def gram(rows, height, slots, total, pieces, extra=None, prev=None, step=1024):
    depth = rows.shape[1]
    n = slots.shape[1]
    width = sum(p.shape[0] for p in pieces)
    fixed = lambda shape: pl.BlockSpec(shape, lambda i, s: (0, 0), pipeline_mode=pl.Buffered(1))
    in_specs = [pl.BlockSpec((height, depth), lambda i, s: (s[0, i], 0))]
    in_specs += [fixed(p.shape) for p in pieces]
    out_specs = [pl.BlockSpec((height, width), lambda i, s: (s[1, i], 0))]
    out_shape = [jax.ShapeDtypeStruct((total * height, width), jnp.float32)]
    args = [rows, *pieces]
    if extra is not None:
        in_specs.insert(0, fixed((EXTRA, depth)))
        out_specs.insert(0, pl.BlockSpec((EXTRA, width), lambda i, s: (0, 0)))
        out_shape.insert(0, jax.ShapeDtypeStruct((EXTRA, width), jnp.float32))
        args.insert(0, extra)
    aliases = {}
    if prev is not None:
        in_specs.append(pl.BlockSpec(memory_space=pl.ANY))
        aliases = {len(args) + 1: 0}
        args.append(prev)
    return pl.pallas_call(
        functools.partial(gram_kernel, extra is not None, step, len(pieces)),
        grid_spec=pltpu.PrefetchScalarGridSpec(
            num_scalar_prefetch=1,
            grid=(n,),
            in_specs=in_specs,
            out_specs=out_specs,
            scratch_shapes=[pltpu.VMEM((width, depth), jnp.bfloat16)],
        ),
        out_shape=out_shape,
        input_output_aliases=aliases,
        cost_estimate=pl.CostEstimate(
            flops=2 * n * height * width * depth,
            bytes_accessed=2 * depth * (n * height + width) + 4 * n * height * width,
            transcendentals=0,
        ),
        name="gram",
    )(slots, *args)


def halves_kernel(pieces, e_ref, a_ref, *refs):
    c_refs = refs[:pieces]
    x_ref, theirs_ref, mine_ref, c_ref = refs[pieces:]
    step, half = pl.program_id(0), pl.num_programs(0) // 2

    @pl.when(step == 0)
    def _():
        at = 0
        for ref in c_refs:
            c_ref[at : at + ref.shape[0], :] = ref[...]
            at += ref.shape[0]

    def dot(a):
        return lax.dot_general(
            a, c_ref[...], (((1,), (1,)), ((), ())), preferred_element_type=jnp.float32
        )

    @pl.when(step < half)
    def _():
        part = dot(jnp.concatenate([e_ref[...], a_ref[...]], axis=0))
        x_ref[...] = part[:EXTRA]
        theirs_ref[...] = part[EXTRA:]

    @pl.when(step >= half)
    def _():
        mine_ref[...] = dot(a_ref[...])


def gram_halves(rows, pieces, extra):
    total, depth = rows.shape
    half = total // 2
    tile = 256 if half % 256 == 0 else half
    n = half // tile
    width = sum(p.shape[0] for p in pieces)
    fixed = lambda shape: pl.BlockSpec(shape, lambda i: (0, 0), pipeline_mode=pl.Buffered(1))
    shape = jax.ShapeDtypeStruct((half, width), jnp.float32)
    return pl.pallas_call(
        functools.partial(halves_kernel, len(pieces)),
        grid=(2 * n,),
        in_specs=[
            fixed((EXTRA, depth)),
            pl.BlockSpec((tile, depth), lambda i: ((i + n) % (2 * n), 0)),
            *[fixed(p.shape) for p in pieces],
        ],
        out_specs=[
            pl.BlockSpec((EXTRA, width), lambda i: (0, 0)),
            pl.BlockSpec((tile, width), lambda i: (jnp.minimum(i, n - 1), 0)),
            pl.BlockSpec((tile, width), lambda i: (jnp.maximum(i - n, 0), 0)),
        ],
        out_shape=[jax.ShapeDtypeStruct((EXTRA, width), jnp.float32), shape, shape],
        scratch_shapes=[pltpu.VMEM((width, depth), jnp.bfloat16)],
        cost_estimate=pl.CostEstimate(
            flops=2 * total * width * depth,
            bytes_accessed=2 * depth * (total + width) + 4 * total * width,
            transcendentals=0,
        ),
        name="gram_halves",
    )(extra, rows, *pieces)


def stage_kernel(pieces, slots_ref, *refs):
    c_refs, w_ref, m_ref = refs[:pieces], refs[pieces], refs[pieces + 1]
    o_ref, l_ref = refs[-2:]
    lanes = l_ref.shape[1]
    for i in range(pieces):

        @pl.when(pl.program_id(0) == i)
        def _():

            def body(c, level):
                at = pl.ds(pl.multiple_of(c * lanes, lanes), lanes)
                value = c_refs[i][:, at].astype(jnp.float32) * w_ref[:, at]
                value = value.astype(jnp.bfloat16)
                o_ref[:, at] = value
                return level + value.astype(jnp.float32) * m_ref[:, at]

            chunks = o_ref.shape[1] // lanes
            level = lax.fori_loop(0, chunks, body, jnp.zeros(l_ref.shape, jnp.float32))
            l_ref[...] = level


def stage(prev, slots, pieces, weight, mean, total):
    height, depth = pieces[0].shape
    n = len(pieces)
    lanes = min(128, depth)
    fixed = lambda shape: pl.BlockSpec(shape, lambda i, _: (0, 0), pipeline_mode=pl.Buffered(1))
    in_specs = [fixed((height, depth)) for _ in pieces] + [fixed((1, depth))] * 2
    args = [slots, *pieces, weight, mean]
    aliases = {}
    if prev is not None:
        aliases = {len(args): 0, len(args) + 1: 1}
        in_specs += [pl.BlockSpec(memory_space=pl.ANY)] * 2
        args += prev
    return pl.pallas_call(
        functools.partial(stage_kernel, n),
        grid_spec=pltpu.PrefetchScalarGridSpec(
            num_scalar_prefetch=1,
            grid=(n,),
            in_specs=in_specs,
            out_specs=[
                pl.BlockSpec((height, depth), lambda i, s: (s[i], 0)),
                pl.BlockSpec((height, lanes), lambda i, s: (s[i], 0)),
            ],
        ),
        out_shape=[
            jax.ShapeDtypeStruct((total, depth), jnp.bfloat16),
            jax.ShapeDtypeStruct((total, lanes), jnp.float32),
        ],
        input_output_aliases=aliases,
        cost_estimate=pl.CostEstimate(
            flops=n * height * depth, bytes_accessed=4 * n * height * depth, transcendentals=0
        ),
        name="stage",
    )(*args)


def place_kernel(parts, info_ref, *refs):
    values, ships = refs[:parts], refs[parts : 2 * parts]
    first_ref, second_ref = refs[-2:]
    width = ships[0].shape[1]
    same, upper = info_ref[2] == 1, info_ref[3] == 1
    for i in range(parts):
        at = slice(i * width, (i + 1) * width)
        a, b = values[i][:, :width], values[i][:, width:]
        keep = jnp.where(same, a, b)
        ship = ships[i][...]
        first_ref[:, at] = jnp.where(upper, ship, keep)
        second_ref[:, at] = jnp.where(upper, keep, ship)


def place(outs, info, values, ships, total):
    count = values[0].shape[0]
    parts = len(values)
    width = ships[0].shape[1]
    tile = count // 3 if count % 24 == 0 else count
    in_specs = [pl.BlockSpec((tile, 2 * width), lambda i, _: (i, 0))] * parts
    in_specs += [pl.BlockSpec((tile, width), lambda i, _: (i, 0))] * parts
    args = [info, *values, *ships]
    aliases = {}
    if outs is not None:
        aliases = {len(args): 0, len(args) + 1: 1}
        in_specs += [pl.BlockSpec(memory_space=pl.ANY)] * 2
        args += outs
    shape = jax.ShapeDtypeStruct((count, total), jnp.float32)
    return pl.pallas_call(
        functools.partial(place_kernel, parts),
        grid_spec=pltpu.PrefetchScalarGridSpec(
            num_scalar_prefetch=1,
            grid=(count // tile,),
            in_specs=in_specs,
            out_specs=[
                pl.BlockSpec((tile, parts * width), lambda i, s: (i, s[0])),
                pl.BlockSpec((tile, parts * width), lambda i, s: (i, s[1])),
            ],
        ),
        out_shape=[shape, shape],
        input_output_aliases=aliases,
        cost_estimate=pl.CostEstimate(
            flops=4 * count * width * parts,
            bytes_accessed=18 * count * width * parts,
            transcendentals=0,
        ),
        name="place",
    )(*args)


def split(x):
    parts = []
    for _ in range(3):
        part = lax.reduce_precision(x, 8, 7)
        parts.append(part.astype(jnp.bfloat16))
        x = x - part
    pad = jnp.zeros((EXTRA - 3,) + x.shape, jnp.bfloat16)
    return jnp.concatenate([jnp.stack(parts), pad])


def per_device(frames, drift):
    local_frames, _, tile_rows, columns = frames.shape
    nt, nc, npix = (lax.axis_size(a) for a in ("trow", "tcol", "pix"))
    assert nt == 4 and nc == 4
    total_frames = local_frames * nt * nc
    pixels = tile_rows * columns
    band_pixels = pixels * npix
    t, z, pix = (lax.axis_index(a) for a in ("trow", "tcol", "pix"))
    upper = z >= 2
    at_end = (z == 0) | (z == nc - 1)
    beta = upper.astype(jnp.int32)
    height = local_frames // PIECES

    head, tail = edges(frames)
    lo = lax.ppermute(tail, "pix", [(i, i + 1) for i in range(npix - 1)])
    hi = lax.ppermute(head, "pix", [(i + 1, i) for i in range(npix - 1)])
    parts = [shift(beta[None], frames, lo, hi, drift, i * height, height) for i in range(PIECES)]
    band0, band1, own, sums = ([part[j] for part in parts] for j in range(4))

    total = sum(sums).reshape(2, tile_rows, 8, columns).sum(axis=2)
    for axis, step in (("trow", 1), ("trow", 2), ("tcol", 1), ("tcol", 2)):
        total = total + lax.ppermute(total, axis, [(i, i ^ step) for i in range(4)])
    mean = (jnp.where(upper, total[1], total[0]) / total_frames).reshape(pixels)
    weight = 1.0 / (mean * mean)

    down = [(i + 1, i) for i in range(nc - 1)]
    upward = [(i, i + 1) for i in range(nc - 1)]
    outward = [(1, 0), (2, 3)]
    down1 = [lax.ppermute(band0[i], "tcol", down) for i in range(PIECES)]
    up1 = [lax.ppermute(band1[i], "tcol", upward) for i in range(PIECES)]
    first, second, third, down2, up2 = [], [], [], [], []
    for i in range(PIECES):
        first.append(jnp.where(upper, up1[i], down1[i]))
        payload = jnp.where(z == nc - 1, band1[i], down1[i])
        down2.append(lax.ppermute(payload, "tcol", down))
        payload = jnp.where(z == 0, band0[i], up1[i])
        up2.append(lax.ppermute(payload, "tcol", upward))
    for i in range(PIECES):
        second.append(jnp.where(upper, up2[i], down2[i]))
        moved = lax.ppermute(second[i], "tcol", outward)
        third.append(jnp.where(at_end, moved, jnp.where(upper, down2[i], up2[i])))
    stream = own + first + second + third
    blocks = [[0, 1, 2, 3], [1, 2, 3, 0], [2, 1, 0, 3], [3, 2, 1, 0]]
    half = nc // 2
    table = []
    for zz in range(nc):
        for pp in range(npix):
            slots = list(blocks[zz])
            if npix == 2:
                slots = [((b // half) ^ pp) * half + b % half for b in slots]
            line = [b * PIECES + i for b in slots for i in range(PIECES)] + slots
            for k in range(nc):
                line += [blocks[zz if band == zz // half else zz ^ half][k] for band in range(2)]
            table.append(line)
    table = jnp.array(table, jnp.int32)
    same = (t & 2) == (z & 2)
    line = lax.dynamic_slice(table, (z * npix + pix, 0), (1, table.shape[1]))[0]
    flags = jnp.stack([same, upper]).astype(jnp.int32)

    index = lambda a, b: a * nc + b
    across = [
        (index(a, b), index(a ^ 1, b)) for a in range(nt) for b in range(nc) if (a & 1) == (b & 1)
    ]
    swap = [(index(a, b), index(a ^ 2, b)) for a in range(nt) for b in range(nc)]
    source = (t & 1) == (z & 1)
    near, far = [], []
    for k, piece in enumerate(stream):
        got = lax.ppermute(piece, GRID, across)
        near.append(jnp.where(source, piece, got))
        far.append(lax.ppermute(near[-1], GRID, swap))

    staged = None
    for k in range(nc):
        at = slice(k * PIECES, (k + 1) * PIECES)
        scale, *block, _ = lax.optimization_barrier((weight, *stream[at], far[0]))
        staged = stage(staged, line[at], block, scale[None], mean[None], nc * local_frames)
        if k == nc - 2:
            early = staged[0]
    rows, level = staged
    level = level.sum(axis=1)
    count = nc * local_frames // npix
    if npix == 2:
        level = level[:count] + lax.ppermute(level[count:], "pix", [(0, 1), (1, 0)])
    else:
        level = lax.psum_scatter(level, "pix", scatter_dimension=0, tiled=True)
    row_scale = band_pixels / level
    extra = split(1.0 / mean)
    order = line[nc * PIECES : nc * PIECES + nc]
    order = jnp.stack([order, order])
    everything = nc * local_frames
    tile = 256 if count % 256 == 0 else local_frames
    tiles = lambda start, n: jnp.array([range(start, start + n), range(n)], jnp.int32)

    def correlate(name, cols, gate, ahead):
        other_core = [(0, 1), (1, 0)]
        if npix == 2 and ahead:
            slots = order[:, : nc - 1]
            sums, part = gram(early, local_frames, slots, nc, cols, extra, step=256)
            slots = order[:, nc - 1 :]
            (part,) = gram(rows, local_frames, slots, nc, cols, prev=part, step=384)
            total, theirs = part[:count], lax.ppermute(part[count:], "pix", other_core)
        elif npix == 2 and name == 2:
            n = count // tile
            sums, theirs = gram(rows, tile, tiles(n, n), n, cols, extra)
            theirs = lax.ppermute(theirs, "pix", other_core)
            (total,) = gram(rows, tile, tiles(0, n), n, cols)
        elif npix == 2:
            sums, theirs, total = gram_halves(rows, cols, extra)
            theirs = lax.ppermute(theirs, "pix", other_core)
        else:
            n = everything // tile
            sums, part = gram(rows, tile, tiles(0, n), n, cols, extra)
            total = lax.psum_scatter(part, "pix", scatter_dimension=0, tiled=True)
            theirs = jnp.zeros_like(total)
        sums = sums[:3].sum(axis=0)
        if npix == 2:
            sums = sums + lax.ppermute(sums, "pix", other_core)
        else:
            sums = lax.psum(sums, "pix")
        theirs, gate = lax.optimization_barrier((theirs, gate))
        return (total + theirs) * row_scale[:, None] * (1.0 / sums)[None, :]

    over = [(i, i ^ 2) for i in range(nc)]
    chunks = [[(k, 0, PIECES)] for k in range(nc - 1)] + [[(nc - 1, i, 1) for i in range(PIECES)]]
    gate, outs, n = row_scale, None, 0
    for parts in chunks:
        values, ships = [], []
        for k, i, size in parts:
            lo = k * PIECES + i
            value = correlate(n, near[lo : lo + size] + far[lo : lo + size], gate, k < 2)
            a, b = value[:, : size * height], value[:, size * height :]
            gate = (jnp.where(same, b, a) - 1.0).astype(SHIP)
            values.append(value)
            ships.append(lax.ppermute(gate, "tcol", over).astype(jnp.float32) + 1.0)
            n += 1
        at = nc * PIECES + nc + 2 * k
        info = jnp.concatenate([line[at : at + 2], flags])
        outs = place(outs, info, values, ships, nc * local_frames)
    return outs[0], outs[1]


def solution(mesh):
    in_specs = (P(("trow", "tcol"), None, "pix", None), P(("trow", "tcol"), None))
    out_specs = (P(("trow", "pix"), "tcol"), P(("trow", "pix"), "tcol"))

    return jax.shard_map(
        per_device, mesh=mesh, in_specs=in_specs, out_specs=out_specs, check_vma=False
    )
```

```python
import functools

import jax
import jax.numpy as jnp
from jax import lax
from jax.experimental import pallas as pl
from jax.experimental.pallas import tpu as pltpu
from jax.sharding import PartitionSpec as P


PIECES = 2
SHIP = jnp.float16
EXTRA = 16
GRID = ("trow", "tcol")


def edge_kernel(parts, *refs):
    head_ref, tail_ref = refs[-2:]
    for n, ref in enumerate(refs[:-2]):
        f, _, rows, cols = ref.shape
        band, rest = divmod(n, 2 * parts)
        part, last = divmod(rest, 2)
        flat = ref.reshape(f * rows, cols)
        value = flat[pl.ds(rows - 1 if last else 0, f, stride=rows), :].astype(jnp.bfloat16)
        (tail_ref if last else head_ref)[band, part * f : (part + 1) * f, :] = value


def edges(frames):
    n, bands, rows, cols = frames.shape
    group = min(8, rows)
    parts = 2
    specs = []
    for band in range(bands):
        for part in range(parts):
            for block in (0, rows // group - 1):
                at = (part, band, block, 0)
                specs.append(pl.BlockSpec((n // parts, 1, group, cols), lambda i, at=at: at))
    out = pl.BlockSpec((bands, n, cols), lambda i: (0, 0, 0))
    shape = jax.ShapeDtypeStruct((bands, n, cols), jnp.bfloat16)
    return pl.pallas_call(
        functools.partial(edge_kernel, parts),
        grid=(1,),
        in_specs=specs,
        out_specs=[out, out],
        out_shape=[shape, shape],
        name="edges",
    )(*[frames] * len(specs))


def shift_kernel(beta_ref, x_ref, lo_ref, hi_ref, d_ref, s0_ref, s1_ref, own_ref, sum_ref):
    frames, bands, rows, cols = x_ref.shape
    f = 16 if frames % 16 == 0 else frames
    flat = x_ref.reshape(frames * bands * rows, cols)

    @pl.when(pl.program_id(0) == 0)
    def _():
        sum_ref[...] = jnp.zeros_like(sum_ref)

    @pl.loop(0, frames // f)
    def _(g):
        base = pl.multiple_of(g * f, f)
        group = pl.ds(base, f)
        steps = d_ref[group, :]

        def share(v):
            return jnp.broadcast_to(v.astype(jnp.float32) * 0.125, (f, cols))

        lane = lax.broadcasted_iota(jnp.int32, (f, cols), 1)
        by_row, by_col = steps[:, 0:1], steps[:, 1:2]
        up, down = share(jnp.maximum(by_row, 0)), share(jnp.maximum(-by_row, 0))
        stay = 1.0 - up - down
        right, left = share(jnp.maximum(by_col, 0)), share(jnp.maximum(-by_col, 0))
        keep = 1.0 - right - left
        right = jnp.where(lane == cols - 1, 0.0, right)
        left = jnp.where(lane == 0, 0.0, left)

        for band, s_ref in ((0, s0_ref), (1, s1_ref)):

            def row(r):
                if r < 0:
                    return lo_ref[band, group, :].astype(jnp.float32)
                if r >= rows:
                    return hi_ref[band, group, :].astype(jnp.float32)
                start = base * (bands * rows) + (band * rows + r)
                return flat[pl.ds(start, f, stride=bands * rows), :]

            before, here = row(-1), row(0)
            for r in range(rows):
                after = row(r + 1)
                p = stay * here + up * after + down * before
                s = keep * p + right * pltpu.roll(p, cols - 1, 1) + left * pltpu.roll(p, 1, 1)
                s = s.astype(jnp.bfloat16)
                s_ref[group, r * cols : (r + 1) * cols] = s
                part = jnp.sum(s.astype(jnp.float32).reshape(f // 8, 8, cols), axis=0)
                sum_ref[band, r * 8 : r * 8 + 8, :] += part
                before, here = here, after

    for band, s_ref in ((0, s0_ref), (1, s1_ref)):

        @pl.when(beta_ref[0] == band)
        def _():
            own_ref[...] = s_ref[...]


def shift(beta, frames, lo, hi, drift, start, count):
    _, bands, rows, cols = frames.shape
    fb = count
    while fb > 64 and fb % 2 == 0:
        fb //= 2
    first = start // fb
    edge = pl.BlockSpec((bands, fb, cols), lambda i, _: (0, i + first, 0))
    out = pl.BlockSpec((fb, rows * cols), lambda i, _: (i, 0))
    shape = jax.ShapeDtypeStruct((count, rows * cols), jnp.bfloat16)
    return pl.pallas_call(
        shift_kernel,
        grid_spec=pltpu.PrefetchScalarGridSpec(
            num_scalar_prefetch=1,
            grid=(count // fb,),
            in_specs=[
                pl.BlockSpec((fb, bands, rows, cols), lambda i, _: (i + first, 0, 0, 0)),
                edge,
                edge,
                pl.BlockSpec((fb, 2), lambda i, _: (i + first, 0)),
            ],
            out_specs=[
                out,
                out,
                out,
                pl.BlockSpec((bands, rows * 8, cols), lambda i, _: (0, 0, 0)),
            ],
        ),
        out_shape=[shape, shape, shape, jax.ShapeDtypeStruct((bands, rows * 8, cols), jnp.float32)],
        cost_estimate=pl.CostEstimate(
            flops=count * bands * rows * cols * 12,
            bytes_accessed=count * bands * rows * cols * 7,
            transcendentals=0,
        ),
        name="shift",
    )(beta, frames, lo, hi, drift)


def gram_kernel(extra, step, pieces, slots_ref, *refs):
    refs = list(refs)
    e_ref = refs.pop(0) if extra else None
    a_ref = refs.pop(0)
    c_refs = refs[:pieces]
    o_ref, c_ref = refs[-2:]

    @pl.when(pl.program_id(0) == 0)
    def _():
        at = 0
        for ref in c_refs:
            c_ref[at : at + ref.shape[0], :] = ref[...]
            at += ref.shape[0]

    a = a_ref[...]
    if extra:
        a = jnp.concatenate([e_ref[...], a], axis=0)
    width = o_ref.shape[1]

    def chunk(at):
        part = lax.dot_general(
            a, c_ref[at, :], (((1,), (1,)), ((), ())), preferred_element_type=jnp.float32
        )
        if extra:
            refs[-3][:, at] = part[:EXTRA]
            part = part[EXTRA:]
        o_ref[:, at] = part

    if step < width and width % step == 0:

        @pl.loop(0, width // step)
        def _(j):
            chunk(pl.ds(pl.multiple_of(j * step, step), step))

    else:
        chunk(slice(0, width))


def gram(rows, height, slots, total, pieces, extra=None, prev=None, step=1024):
    depth = rows.shape[1]
    n = slots.shape[1]
    width = sum(p.shape[0] for p in pieces)
    fixed = lambda shape: pl.BlockSpec(shape, lambda i, s: (0, 0), pipeline_mode=pl.Buffered(1))
    in_specs = [pl.BlockSpec((height, depth), lambda i, s: (s[0, i], 0))]
    in_specs += [fixed(p.shape) for p in pieces]
    out_specs = [pl.BlockSpec((height, width), lambda i, s: (s[1, i], 0))]
    out_shape = [jax.ShapeDtypeStruct((total * height, width), jnp.float32)]
    args = [rows, *pieces]
    if extra is not None:
        in_specs.insert(0, fixed((EXTRA, depth)))
        out_specs.insert(0, pl.BlockSpec((EXTRA, width), lambda i, s: (0, 0)))
        out_shape.insert(0, jax.ShapeDtypeStruct((EXTRA, width), jnp.float32))
        args.insert(0, extra)
    aliases = {}
    if prev is not None:
        in_specs.append(pl.BlockSpec(memory_space=pl.ANY))
        aliases = {len(args) + 1: 0}
        args.append(prev)
    return pl.pallas_call(
        functools.partial(gram_kernel, extra is not None, step, len(pieces)),
        grid_spec=pltpu.PrefetchScalarGridSpec(
            num_scalar_prefetch=1,
            grid=(n,),
            in_specs=in_specs,
            out_specs=out_specs,
            scratch_shapes=[pltpu.VMEM((width, depth), jnp.bfloat16)],
        ),
        out_shape=out_shape,
        input_output_aliases=aliases,
        cost_estimate=pl.CostEstimate(
            flops=2 * n * height * width * depth,
            bytes_accessed=2 * depth * (n * height + width) + 4 * n * height * width,
            transcendentals=0,
        ),
        name="gram",
    )(slots, *args)


def halves_kernel(pieces, e_ref, a_ref, *refs):
    c_refs = refs[:pieces]
    x_ref, theirs_ref, mine_ref, c_ref = refs[pieces:]
    step, half = pl.program_id(0), pl.num_programs(0) // 2

    @pl.when(step == 0)
    def _():
        at = 0
        for ref in c_refs:
            c_ref[at : at + ref.shape[0], :] = ref[...]
            at += ref.shape[0]

    def dot(a):
        return lax.dot_general(
            a, c_ref[...], (((1,), (1,)), ((), ())), preferred_element_type=jnp.float32
        )

    @pl.when(step < half)
    def _():
        part = dot(jnp.concatenate([e_ref[...], a_ref[...]], axis=0))
        x_ref[...] = part[:EXTRA]
        theirs_ref[...] = part[EXTRA:]

    @pl.when(step >= half)
    def _():
        mine_ref[...] = dot(a_ref[...])


def gram_halves(rows, pieces, extra):
    total, depth = rows.shape
    half = total // 2
    tile = 256 if half % 256 == 0 else half
    n = half // tile
    width = sum(p.shape[0] for p in pieces)
    fixed = lambda shape: pl.BlockSpec(shape, lambda i: (0, 0), pipeline_mode=pl.Buffered(1))
    shape = jax.ShapeDtypeStruct((half, width), jnp.float32)
    return pl.pallas_call(
        functools.partial(halves_kernel, len(pieces)),
        grid=(2 * n,),
        in_specs=[
            fixed((EXTRA, depth)),
            pl.BlockSpec((tile, depth), lambda i: ((i + n) % (2 * n), 0)),
            *[fixed(p.shape) for p in pieces],
        ],
        out_specs=[
            pl.BlockSpec((EXTRA, width), lambda i: (0, 0)),
            pl.BlockSpec((tile, width), lambda i: (jnp.minimum(i, n - 1), 0)),
            pl.BlockSpec((tile, width), lambda i: (jnp.maximum(i - n, 0), 0)),
        ],
        out_shape=[jax.ShapeDtypeStruct((EXTRA, width), jnp.float32), shape, shape],
        scratch_shapes=[pltpu.VMEM((width, depth), jnp.bfloat16)],
        cost_estimate=pl.CostEstimate(
            flops=2 * total * width * depth,
            bytes_accessed=2 * depth * (total + width) + 4 * total * width,
            transcendentals=0,
        ),
        name="gram_halves",
    )(extra, rows, *pieces)


def stage_kernel(pieces, slots_ref, *refs):
    c_refs, w_ref, m_ref = refs[:pieces], refs[pieces], refs[pieces + 1]
    o_ref, l_ref = refs[-2:]
    lanes = l_ref.shape[1]
    for i in range(pieces):

        @pl.when(pl.program_id(0) == i)
        def _():

            def body(c, level):
                at = pl.ds(pl.multiple_of(c * lanes, lanes), lanes)
                value = c_refs[i][:, at].astype(jnp.float32) * w_ref[:, at]
                value = value.astype(jnp.bfloat16)
                o_ref[:, at] = value
                return level + value.astype(jnp.float32) * m_ref[:, at]

            chunks = o_ref.shape[1] // lanes
            unroll = 4 if chunks % 4 == 0 else 1
            level = jnp.zeros(l_ref.shape, jnp.float32)
            level = lax.fori_loop(0, chunks, body, level, unroll=unroll)
            l_ref[...] = level


def stage(prev, slots, pieces, weight, mean, total):
    height, depth = pieces[0].shape
    n = len(pieces)
    lanes = min(128, depth)
    fixed = lambda shape: pl.BlockSpec(shape, lambda i, _: (0, 0), pipeline_mode=pl.Buffered(1))
    in_specs = [fixed((height, depth)) for _ in pieces] + [fixed((1, depth))] * 2
    args = [slots, *pieces, weight, mean]
    aliases = {}
    if prev is not None:
        aliases = {len(args): 0, len(args) + 1: 1}
        in_specs += [pl.BlockSpec(memory_space=pl.ANY)] * 2
        args += prev
    return pl.pallas_call(
        functools.partial(stage_kernel, n),
        grid_spec=pltpu.PrefetchScalarGridSpec(
            num_scalar_prefetch=1,
            grid=(n,),
            in_specs=in_specs,
            out_specs=[
                pl.BlockSpec((height, depth), lambda i, s: (s[i], 0)),
                pl.BlockSpec((height, lanes), lambda i, s: (s[i], 0)),
            ],
        ),
        out_shape=[
            jax.ShapeDtypeStruct((total, depth), jnp.bfloat16),
            jax.ShapeDtypeStruct((total, lanes), jnp.float32),
        ],
        input_output_aliases=aliases,
        cost_estimate=pl.CostEstimate(
            flops=n * height * depth, bytes_accessed=4 * n * height * depth, transcendentals=0
        ),
        name="stage",
    )(*args)


def place_kernel(parts, info_ref, *refs):
    values, ships = refs[:parts], refs[parts : 2 * parts]
    first_ref, second_ref = refs[-2:]
    width = ships[0].shape[1]
    same, upper = info_ref[2] == 1, info_ref[3] == 1
    for i in range(parts):
        at = slice(i * width, (i + 1) * width)
        a, b = values[i][:, :width], values[i][:, width:]
        keep = jnp.where(same, a, b)
        ship = ships[i][...]
        first_ref[:, at] = jnp.where(upper, ship, keep)
        second_ref[:, at] = jnp.where(upper, keep, ship)


def place(outs, info, values, ships, total):
    count = values[0].shape[0]
    parts = len(values)
    width = ships[0].shape[1]
    tile = count // 3 if count % 24 == 0 else count
    in_specs = [pl.BlockSpec((tile, 2 * width), lambda i, _: (i, 0))] * parts
    in_specs += [pl.BlockSpec((tile, width), lambda i, _: (i, 0))] * parts
    args = [info, *values, *ships]
    aliases = {}
    if outs is not None:
        aliases = {len(args): 0, len(args) + 1: 1}
        in_specs += [pl.BlockSpec(memory_space=pl.ANY)] * 2
        args += outs
    shape = jax.ShapeDtypeStruct((count, total), jnp.float32)
    return pl.pallas_call(
        functools.partial(place_kernel, parts),
        grid_spec=pltpu.PrefetchScalarGridSpec(
            num_scalar_prefetch=1,
            grid=(count // tile,),
            in_specs=in_specs,
            out_specs=[
                pl.BlockSpec((tile, parts * width), lambda i, s: (i, s[0])),
                pl.BlockSpec((tile, parts * width), lambda i, s: (i, s[1])),
            ],
        ),
        out_shape=[shape, shape],
        input_output_aliases=aliases,
        cost_estimate=pl.CostEstimate(
            flops=4 * count * width * parts,
            bytes_accessed=18 * count * width * parts,
            transcendentals=0,
        ),
        name="place",
    )(*args)


def split(x):
    parts = []
    for _ in range(3):
        part = lax.reduce_precision(x, 8, 7)
        parts.append(part.astype(jnp.bfloat16))
        x = x - part
    pad = jnp.zeros((EXTRA - 3,) + x.shape, jnp.bfloat16)
    return jnp.concatenate([jnp.stack(parts), pad])


def per_device(frames, drift):
    local_frames, _, tile_rows, columns = frames.shape
    nt, nc, npix = (lax.axis_size(a) for a in ("trow", "tcol", "pix"))
    assert nt == 4 and nc == 4
    total_frames = local_frames * nt * nc
    pixels = tile_rows * columns
    band_pixels = pixels * npix
    t, z, pix = (lax.axis_index(a) for a in ("trow", "tcol", "pix"))
    upper = z >= 2
    at_end = (z == 0) | (z == nc - 1)
    beta = upper.astype(jnp.int32)
    height = local_frames // PIECES

    head, tail = edges(frames)
    lo = lax.ppermute(tail, "pix", [(i, i + 1) for i in range(npix - 1)])
    hi = lax.ppermute(head, "pix", [(i + 1, i) for i in range(npix - 1)])
    parts = [shift(beta[None], frames, lo, hi, drift, i * height, height) for i in range(PIECES)]
    band0, band1, own, sums = ([part[j] for part in parts] for j in range(4))

    total = sum(sums).reshape(2, tile_rows, 8, columns).sum(axis=2)
    for axis, step in (("trow", 1), ("trow", 2), ("tcol", 1), ("tcol", 2)):
        total = total + lax.ppermute(total, axis, [(i, i ^ step) for i in range(4)])
    mean = (jnp.where(upper, total[1], total[0]) / total_frames).reshape(pixels)
    weight = 1.0 / (mean * mean)

    down = [(i + 1, i) for i in range(nc - 1)]
    upward = [(i, i + 1) for i in range(nc - 1)]
    outward = [(1, 0), (2, 3)]
    down1 = [lax.ppermute(band0[i], "tcol", down) for i in range(PIECES)]
    up1 = [lax.ppermute(band1[i], "tcol", upward) for i in range(PIECES)]
    first, second, third, down2, up2 = [], [], [], [], []
    for i in range(PIECES):
        first.append(jnp.where(upper, up1[i], down1[i]))
        payload = jnp.where(z == nc - 1, band1[i], down1[i])
        down2.append(lax.ppermute(payload, "tcol", down))
        payload = jnp.where(z == 0, band0[i], up1[i])
        up2.append(lax.ppermute(payload, "tcol", upward))
    for i in range(PIECES):
        second.append(jnp.where(upper, up2[i], down2[i]))
        moved = lax.ppermute(second[i], "tcol", outward)
        third.append(jnp.where(at_end, moved, jnp.where(upper, down2[i], up2[i])))
    stream = own + first + second + third
    blocks = [[0, 1, 2, 3], [1, 2, 3, 0], [2, 1, 0, 3], [3, 2, 1, 0]]
    half = nc // 2
    table = []
    for zz in range(nc):
        for pp in range(npix):
            slots = list(blocks[zz])
            if npix == 2:
                slots = [((b // half) ^ pp) * half + b % half for b in slots]
            line = [b * PIECES + i for b in slots for i in range(PIECES)] + slots
            for k in range(nc):
                line += [blocks[zz if band == zz // half else zz ^ half][k] for band in range(2)]
            table.append(line)
    table = jnp.array(table, jnp.int32)
    same = (t & 2) == (z & 2)
    line = lax.dynamic_slice(table, (z * npix + pix, 0), (1, table.shape[1]))[0]
    flags = jnp.stack([same, upper]).astype(jnp.int32)

    index = lambda a, b: a * nc + b
    across = [
        (index(a, b), index(a ^ 1, b)) for a in range(nt) for b in range(nc) if (a & 1) == (b & 1)
    ]
    swap = [(index(a, b), index(a ^ 2, b)) for a in range(nt) for b in range(nc)]
    source = (t & 1) == (z & 1)
    near, far = [], []
    for k, piece in enumerate(stream):
        got = lax.ppermute(piece, GRID, across)
        near.append(jnp.where(source, piece, got))
        far.append(lax.ppermute(near[-1], GRID, swap))

    staged = None
    for k in range(nc):
        at = slice(k * PIECES, (k + 1) * PIECES)
        scale, *block, _ = lax.optimization_barrier((weight, *stream[at], far[0]))
        staged = stage(staged, line[at], block, scale[None], mean[None], nc * local_frames)
        if k == nc - 2:
            early = staged[0]
    rows, level = staged
    level = level.sum(axis=1)
    count = nc * local_frames // npix
    if npix == 2:
        level = level[:count] + lax.ppermute(level[count:], "pix", [(0, 1), (1, 0)])
    else:
        level = lax.psum_scatter(level, "pix", scatter_dimension=0, tiled=True)
    row_scale = band_pixels / level
    extra = split(1.0 / mean)
    order = line[nc * PIECES : nc * PIECES + nc]
    order = jnp.stack([order, order])
    everything = nc * local_frames
    tile = 256 if count % 256 == 0 else local_frames
    tiles = lambda start, n: jnp.array([range(start, start + n), range(n)], jnp.int32)

    def correlate(name, cols, gate, ahead):
        other_core = [(0, 1), (1, 0)]
        if npix == 2 and ahead:
            slots = order[:, : nc - 1]
            sums, part = gram(early, local_frames, slots, nc, cols, extra, step=256)
            slots = order[:, nc - 1 :]
            step = 1024 if name == 0 else 384
            (part,) = gram(rows, local_frames, slots, nc, cols, prev=part, step=step)
            total, theirs = part[:count], lax.ppermute(part[count:], "pix", other_core)
        elif npix == 2 and name == 2:
            n = count // tile
            sums, theirs = gram(rows, tile, tiles(n, n), n, cols, extra)
            theirs = lax.ppermute(theirs, "pix", other_core)
            (total,) = gram(rows, tile, tiles(0, n), n, cols)
        elif npix == 2:
            sums, theirs, total = gram_halves(rows, cols, extra)
            theirs = lax.ppermute(theirs, "pix", other_core)
        else:
            n = everything // tile
            sums, part = gram(rows, tile, tiles(0, n), n, cols, extra)
            total = lax.psum_scatter(part, "pix", scatter_dimension=0, tiled=True)
            theirs = jnp.zeros_like(total)
        sums = sums[:3].sum(axis=0)
        if npix == 2:
            sums = sums + lax.ppermute(sums, "pix", other_core)
        else:
            sums = lax.psum(sums, "pix")
        theirs, gate = lax.optimization_barrier((theirs, gate))
        return (total + theirs) * row_scale[:, None] * (1.0 / sums)[None, :]

    over = [(i, i ^ 2) for i in range(nc)]
    chunks = [[(k, 0, PIECES)] for k in range(nc - 1)] + [[(nc - 1, i, 1) for i in range(PIECES)]]
    gate, outs, n = row_scale, None, 0
    for parts in chunks:
        values, ships = [], []
        for k, i, size in parts:
            lo = k * PIECES + i
            value = correlate(n, near[lo : lo + size] + far[lo : lo + size], gate, k < 2)
            a, b = value[:, : size * height], value[:, size * height :]
            gate = (jnp.where(same, b, a) - 1.0).astype(SHIP)
            values.append(value)
            ships.append(lax.ppermute(gate, "tcol", over).astype(jnp.float32) + 1.0)
            n += 1
        at = nc * PIECES + nc + 2 * k
        info = jnp.concatenate([line[at : at + 2], flags])
        outs = place(outs, info, values, ships, nc * local_frames)
    return outs[0], outs[1]


def solution(mesh):
    in_specs = (P(("trow", "tcol"), None, "pix", None), P(("trow", "tcol"), None))
    out_specs = (P(("trow", "pix"), "tcol"), P(("trow", "pix"), "tcol"))

    return jax.shard_map(
        per_device, mesh=mesh, in_specs=in_specs, out_specs=out_specs, check_vma=False
    )
```

```python
import functools

import jax
import jax.numpy as jnp
from jax import lax
from jax.experimental import pallas as pl
from jax.experimental.pallas import tpu as pltpu
from jax.sharding import PartitionSpec as P


PIECES = 2
SHIP = jnp.float16
EXTRA = 16
GRID = ("trow", "tcol")


def edge_kernel(parts, *refs):
    head_ref, tail_ref = refs[-2:]
    for n, ref in enumerate(refs[:-2]):
        f, _, rows, cols = ref.shape
        band, rest = divmod(n, 2 * parts)
        part, last = divmod(rest, 2)
        flat = ref.reshape(f * rows, cols)
        value = flat[pl.ds(rows - 1 if last else 0, f, stride=rows), :].astype(jnp.bfloat16)
        (tail_ref if last else head_ref)[band, part * f : (part + 1) * f, :] = value


def edges(frames):
    n, bands, rows, cols = frames.shape
    group = min(8, rows)
    parts = 2
    specs = []
    for band in range(bands):
        for part in range(parts):
            for block in (0, rows // group - 1):
                at = (part, band, block, 0)
                specs.append(pl.BlockSpec((n // parts, 1, group, cols), lambda i, at=at: at))
    out = pl.BlockSpec((bands, n, cols), lambda i: (0, 0, 0))
    shape = jax.ShapeDtypeStruct((bands, n, cols), jnp.bfloat16)
    return pl.pallas_call(
        functools.partial(edge_kernel, parts),
        grid=(1,),
        in_specs=specs,
        out_specs=[out, out],
        out_shape=[shape, shape],
        name="edges",
    )(*[frames] * len(specs))


def shift_kernel(beta_ref, x_ref, lo_ref, hi_ref, d_ref, s0_ref, s1_ref, own_ref, sum_ref):
    frames, bands, rows, cols = x_ref.shape
    f = 16 if frames % 16 == 0 else frames
    flat = x_ref.reshape(frames * bands * rows, cols)

    @pl.when(pl.program_id(0) == 0)
    def _():
        sum_ref[...] = jnp.zeros_like(sum_ref)

    @pl.loop(0, frames // f)
    def _(g):
        base = pl.multiple_of(g * f, f)
        group = pl.ds(base, f)
        steps = d_ref[group, :]

        def share(v):
            return jnp.broadcast_to(v.astype(jnp.float32) * 0.125, (f, cols))

        lane = lax.broadcasted_iota(jnp.int32, (f, cols), 1)
        by_row, by_col = steps[:, 0:1], steps[:, 1:2]
        up, down = share(jnp.maximum(by_row, 0)), share(jnp.maximum(-by_row, 0))
        stay = 1.0 - up - down
        right, left = share(jnp.maximum(by_col, 0)), share(jnp.maximum(-by_col, 0))
        keep = 1.0 - right - left
        right = jnp.where(lane == cols - 1, 0.0, right)
        left = jnp.where(lane == 0, 0.0, left)

        for band, s_ref in ((0, s0_ref), (1, s1_ref)):

            def row(r):
                if r < 0:
                    return lo_ref[band, group, :].astype(jnp.float32)
                if r >= rows:
                    return hi_ref[band, group, :].astype(jnp.float32)
                start = base * (bands * rows) + (band * rows + r)
                return flat[pl.ds(start, f, stride=bands * rows), :]

            before, here = row(-1), row(0)
            for r in range(rows):
                after = row(r + 1)
                p = stay * here + up * after + down * before
                s = keep * p + right * pltpu.roll(p, cols - 1, 1) + left * pltpu.roll(p, 1, 1)
                s = s.astype(jnp.bfloat16)
                s_ref[group, r * cols : (r + 1) * cols] = s
                part = jnp.sum(s.astype(jnp.float32).reshape(f // 8, 8, cols), axis=0)
                sum_ref[band, r * 8 : r * 8 + 8, :] += part
                before, here = here, after

    for band, s_ref in ((0, s0_ref), (1, s1_ref)):

        @pl.when(beta_ref[0] == band)
        def _():
            own_ref[...] = s_ref[...]


def shift(beta, frames, lo, hi, drift, start, count):
    _, bands, rows, cols = frames.shape
    fb = count
    while fb > 64 and fb % 2 == 0:
        fb //= 2
    first = start // fb
    edge = pl.BlockSpec((bands, fb, cols), lambda i, _: (0, i + first, 0))
    out = pl.BlockSpec((fb, rows * cols), lambda i, _: (i, 0))
    shape = jax.ShapeDtypeStruct((count, rows * cols), jnp.bfloat16)
    return pl.pallas_call(
        shift_kernel,
        grid_spec=pltpu.PrefetchScalarGridSpec(
            num_scalar_prefetch=1,
            grid=(count // fb,),
            in_specs=[
                pl.BlockSpec((fb, bands, rows, cols), lambda i, _: (i + first, 0, 0, 0)),
                edge,
                edge,
                pl.BlockSpec((fb, 2), lambda i, _: (i + first, 0)),
            ],
            out_specs=[
                out,
                out,
                out,
                pl.BlockSpec((bands, rows * 8, cols), lambda i, _: (0, 0, 0)),
            ],
        ),
        out_shape=[shape, shape, shape, jax.ShapeDtypeStruct((bands, rows * 8, cols), jnp.float32)],
        cost_estimate=pl.CostEstimate(
            flops=count * bands * rows * cols * 12,
            bytes_accessed=count * bands * rows * cols * 7,
            transcendentals=0,
        ),
        name="shift",
    )(beta, frames, lo, hi, drift)


def gram_kernel(extra, step, pieces, slots_ref, *refs):
    refs = list(refs)
    e_ref = refs.pop(0) if extra else None
    a_ref = refs.pop(0)
    c_refs = refs[:pieces]
    o_ref, c_ref = refs[-2:]

    @pl.when(pl.program_id(0) == 0)
    def _():
        at = 0
        for ref in c_refs:
            c_ref[at : at + ref.shape[0], :] = ref[...]
            at += ref.shape[0]

    a = a_ref[...]
    if extra:
        a = jnp.concatenate([e_ref[...], a], axis=0)
    width = o_ref.shape[1]

    def chunk(at):
        part = lax.dot_general(
            a, c_ref[at, :], (((1,), (1,)), ((), ())), preferred_element_type=jnp.float32
        )
        if extra:
            refs[-3][:, at] = part[:EXTRA]
            part = part[EXTRA:]
        o_ref[:, at] = part

    if step < width and width % step == 0:

        @pl.loop(0, width // step)
        def _(j):
            chunk(pl.ds(pl.multiple_of(j * step, step), step))

    else:
        chunk(slice(0, width))


def gram(rows, height, slots, total, pieces, extra=None, prev=None, step=1024):
    depth = rows.shape[1]
    n = slots.shape[1]
    width = sum(p.shape[0] for p in pieces)
    fixed = lambda shape: pl.BlockSpec(shape, lambda i, s: (0, 0), pipeline_mode=pl.Buffered(1))
    in_specs = [pl.BlockSpec((height, depth), lambda i, s: (s[0, i], 0))]
    in_specs += [fixed(p.shape) for p in pieces]
    out_specs = [pl.BlockSpec((height, width), lambda i, s: (s[1, i], 0))]
    out_shape = [jax.ShapeDtypeStruct((total * height, width), jnp.float32)]
    args = [rows, *pieces]
    if extra is not None:
        in_specs.insert(0, fixed((EXTRA, depth)))
        out_specs.insert(0, pl.BlockSpec((EXTRA, width), lambda i, s: (0, 0)))
        out_shape.insert(0, jax.ShapeDtypeStruct((EXTRA, width), jnp.float32))
        args.insert(0, extra)
    aliases = {}
    if prev is not None:
        in_specs.append(pl.BlockSpec(memory_space=pl.ANY))
        aliases = {len(args) + 1: 0}
        args.append(prev)
    return pl.pallas_call(
        functools.partial(gram_kernel, extra is not None, step, len(pieces)),
        grid_spec=pltpu.PrefetchScalarGridSpec(
            num_scalar_prefetch=1,
            grid=(n,),
            in_specs=in_specs,
            out_specs=out_specs,
            scratch_shapes=[pltpu.VMEM((width, depth), jnp.bfloat16)],
        ),
        out_shape=out_shape,
        input_output_aliases=aliases,
        cost_estimate=pl.CostEstimate(
            flops=2 * n * height * width * depth,
            bytes_accessed=2 * depth * (n * height + width) + 4 * n * height * width,
            transcendentals=0,
        ),
        name="gram",
    )(slots, *args)


def halves_kernel(pieces, e_ref, a_ref, *refs):
    c_refs = refs[:pieces]
    x_ref, theirs_ref, mine_ref, c_ref = refs[pieces:]
    step, half = pl.program_id(0), pl.num_programs(0) // 2

    @pl.when(step == 0)
    def _():
        at = 0
        for ref in c_refs:
            c_ref[at : at + ref.shape[0], :] = ref[...]
            at += ref.shape[0]

    def dot(a):
        return lax.dot_general(
            a, c_ref[...], (((1,), (1,)), ((), ())), preferred_element_type=jnp.float32
        )

    @pl.when(step < half)
    def _():
        part = dot(jnp.concatenate([e_ref[...], a_ref[...]], axis=0))
        x_ref[...] = part[:EXTRA]
        theirs_ref[...] = part[EXTRA:]

    @pl.when(step >= half)
    def _():
        mine_ref[...] = dot(a_ref[...])


def gram_halves(rows, pieces, extra):
    total, depth = rows.shape
    half = total // 2
    tile = 256 if half % 256 == 0 else half
    n = half // tile
    width = sum(p.shape[0] for p in pieces)
    fixed = lambda shape: pl.BlockSpec(shape, lambda i: (0, 0), pipeline_mode=pl.Buffered(1))
    shape = jax.ShapeDtypeStruct((half, width), jnp.float32)
    return pl.pallas_call(
        functools.partial(halves_kernel, len(pieces)),
        grid=(2 * n,),
        in_specs=[
            fixed((EXTRA, depth)),
            pl.BlockSpec((tile, depth), lambda i: ((i + n) % (2 * n), 0)),
            *[fixed(p.shape) for p in pieces],
        ],
        out_specs=[
            pl.BlockSpec((EXTRA, width), lambda i: (0, 0)),
            pl.BlockSpec((tile, width), lambda i: (jnp.minimum(i, n - 1), 0)),
            pl.BlockSpec((tile, width), lambda i: (jnp.maximum(i - n, 0), 0)),
        ],
        out_shape=[jax.ShapeDtypeStruct((EXTRA, width), jnp.float32), shape, shape],
        scratch_shapes=[pltpu.VMEM((width, depth), jnp.bfloat16)],
        cost_estimate=pl.CostEstimate(
            flops=2 * total * width * depth,
            bytes_accessed=2 * depth * (total + width) + 4 * total * width,
            transcendentals=0,
        ),
        name="gram_halves",
    )(extra, rows, *pieces)


def stage_kernel(pieces, slots_ref, *refs):
    c_refs, w_ref, m_ref = refs[:pieces], refs[pieces], refs[pieces + 1]
    o_ref, l_ref = refs[-2:]
    lanes = l_ref.shape[1]
    for i in range(pieces):

        @pl.when(pl.program_id(0) == i)
        def _():

            def body(c, level):
                at = pl.ds(pl.multiple_of(c * lanes, lanes), lanes)
                value = c_refs[i][:, at].astype(jnp.float32) * w_ref[:, at]
                value = value.astype(jnp.bfloat16)
                o_ref[:, at] = value
                return level + value.astype(jnp.float32) * m_ref[:, at]

            chunks = o_ref.shape[1] // lanes
            unroll = 4 if chunks % 4 == 0 else 1
            level = jnp.zeros(l_ref.shape, jnp.float32)
            level = lax.fori_loop(0, chunks, body, level, unroll=unroll)
            l_ref[...] = level


def stage(prev, slots, pieces, weight, mean, total):
    height, depth = pieces[0].shape
    n = len(pieces)
    lanes = min(128, depth)
    fixed = lambda shape: pl.BlockSpec(shape, lambda i, _: (0, 0), pipeline_mode=pl.Buffered(1))
    in_specs = [fixed((height, depth)) for _ in pieces] + [fixed((1, depth))] * 2
    args = [slots, *pieces, weight, mean]
    aliases = {}
    if prev is not None:
        aliases = {len(args): 0, len(args) + 1: 1}
        in_specs += [pl.BlockSpec(memory_space=pl.ANY)] * 2
        args += prev
    return pl.pallas_call(
        functools.partial(stage_kernel, n),
        grid_spec=pltpu.PrefetchScalarGridSpec(
            num_scalar_prefetch=1,
            grid=(n,),
            in_specs=in_specs,
            out_specs=[
                pl.BlockSpec((height, depth), lambda i, s: (s[i], 0)),
                pl.BlockSpec((height, lanes), lambda i, s: (s[i], 0)),
            ],
        ),
        out_shape=[
            jax.ShapeDtypeStruct((total, depth), jnp.bfloat16),
            jax.ShapeDtypeStruct((total, lanes), jnp.float32),
        ],
        input_output_aliases=aliases,
        cost_estimate=pl.CostEstimate(
            flops=n * height * depth, bytes_accessed=4 * n * height * depth, transcendentals=0
        ),
        name="stage",
    )(*args)


def place_kernel(parts, info_ref, *refs):
    values, ships = refs[:parts], refs[parts : 2 * parts]
    first_ref, second_ref = refs[-2:]
    width = ships[0].shape[1]
    same, upper = info_ref[2] == 1, info_ref[3] == 1
    for i in range(parts):
        at = slice(i * width, (i + 1) * width)
        a, b = values[i][:, :width], values[i][:, width:]
        keep = jnp.where(same, a, b)
        ship = ships[i][...]
        first_ref[:, at] = jnp.where(upper, ship, keep)
        second_ref[:, at] = jnp.where(upper, keep, ship)


def place(outs, info, values, ships, total):
    count = values[0].shape[0]
    parts = len(values)
    width = ships[0].shape[1]
    tile = count // 3 if count % 24 == 0 else count
    in_specs = [pl.BlockSpec((tile, 2 * width), lambda i, _: (i, 0))] * parts
    in_specs += [pl.BlockSpec((tile, width), lambda i, _: (i, 0))] * parts
    args = [info, *values, *ships]
    aliases = {}
    if outs is not None:
        aliases = {len(args): 0, len(args) + 1: 1}
        in_specs += [pl.BlockSpec(memory_space=pl.ANY)] * 2
        args += outs
    shape = jax.ShapeDtypeStruct((count, total), jnp.float32)
    return pl.pallas_call(
        functools.partial(place_kernel, parts),
        grid_spec=pltpu.PrefetchScalarGridSpec(
            num_scalar_prefetch=1,
            grid=(count // tile,),
            in_specs=in_specs,
            out_specs=[
                pl.BlockSpec((tile, parts * width), lambda i, s: (i, s[0])),
                pl.BlockSpec((tile, parts * width), lambda i, s: (i, s[1])),
            ],
        ),
        out_shape=[shape, shape],
        input_output_aliases=aliases,
        cost_estimate=pl.CostEstimate(
            flops=4 * count * width * parts,
            bytes_accessed=18 * count * width * parts,
            transcendentals=0,
        ),
        name="place",
    )(*args)


def split(x):
    parts = []
    for _ in range(3):
        part = lax.reduce_precision(x, 8, 7)
        parts.append(part.astype(jnp.bfloat16))
        x = x - part
    pad = jnp.zeros((EXTRA - 3,) + x.shape, jnp.bfloat16)
    return jnp.concatenate([jnp.stack(parts), pad])


def per_device(frames, drift):
    local_frames, _, tile_rows, columns = frames.shape
    nt, nc, npix = (lax.axis_size(a) for a in ("trow", "tcol", "pix"))
    assert nt == 4 and nc == 4
    total_frames = local_frames * nt * nc
    pixels = tile_rows * columns
    band_pixels = pixels * npix
    t, z, pix = (lax.axis_index(a) for a in ("trow", "tcol", "pix"))
    upper = z >= 2
    at_end = (z == 0) | (z == nc - 1)
    beta = upper.astype(jnp.int32)
    height = local_frames // PIECES

    head, tail = edges(frames)
    lo = lax.ppermute(tail, "pix", [(i, i + 1) for i in range(npix - 1)])
    hi = lax.ppermute(head, "pix", [(i + 1, i) for i in range(npix - 1)])
    parts = [shift(beta[None], frames, lo, hi, drift, i * height, height) for i in range(PIECES)]
    band0, band1, own, sums = ([part[j] for part in parts] for j in range(4))

    total = sum(sums).reshape(2, tile_rows, 8, columns).sum(axis=2)
    for axis, step in (("trow", 1), ("trow", 2), ("tcol", 1), ("tcol", 2)):
        total = total + lax.ppermute(total, axis, [(i, i ^ step) for i in range(4)])
    mean = (jnp.where(upper, total[1], total[0]) / total_frames).reshape(pixels)
    weight = 1.0 / (mean * mean)

    down = [(i + 1, i) for i in range(nc - 1)]
    upward = [(i, i + 1) for i in range(nc - 1)]
    outward = [(1, 0), (2, 3)]
    down1 = [lax.ppermute(band0[i], "tcol", down) for i in range(PIECES)]
    up1 = [lax.ppermute(band1[i], "tcol", upward) for i in range(PIECES)]
    first, second, third, down2, up2 = [], [], [], [], []
    for i in range(PIECES):
        first.append(jnp.where(upper, up1[i], down1[i]))
        payload = jnp.where(z == nc - 1, band1[i], down1[i])
        down2.append(lax.ppermute(payload, "tcol", down))
        payload = jnp.where(z == 0, band0[i], up1[i])
        up2.append(lax.ppermute(payload, "tcol", upward))
    for i in range(PIECES):
        second.append(jnp.where(upper, up2[i], down2[i]))
        moved = lax.ppermute(second[i], "tcol", outward)
        third.append(jnp.where(at_end, moved, jnp.where(upper, down2[i], up2[i])))
    stream = own + first + second + third
    blocks = [[0, 1, 2, 3], [1, 2, 3, 0], [2, 1, 0, 3], [3, 2, 1, 0]]
    half = nc // 2
    table = []
    for zz in range(nc):
        for pp in range(npix):
            slots = list(blocks[zz])
            if npix == 2:
                slots = [((b // half) ^ pp) * half + b % half for b in slots]
            line = [b * PIECES + i for b in slots for i in range(PIECES)] + slots
            for k in range(nc):
                line += [blocks[zz if band == zz // half else zz ^ half][k] for band in range(2)]
            table.append(line)
    table = jnp.array(table, jnp.int32)
    same = (t & 2) == (z & 2)
    line = lax.dynamic_slice(table, (z * npix + pix, 0), (1, table.shape[1]))[0]
    flags = jnp.stack([same, upper]).astype(jnp.int32)

    index = lambda a, b: a * nc + b
    across = [
        (index(a, b), index(a ^ 1, b)) for a in range(nt) for b in range(nc) if (a & 1) == (b & 1)
    ]
    swap = [(index(a, b), index(a ^ 2, b)) for a in range(nt) for b in range(nc)]
    source = (t & 1) == (z & 1)
    near, far = [], []
    for k, piece in enumerate(stream):
        got = lax.ppermute(piece, GRID, across)
        near.append(jnp.where(source, piece, got))
        far.append(lax.ppermute(near[-1], GRID, swap))

    staged = None
    for k in range(nc):
        groups = [[0, 1]] if k < nc - 1 else [[0], [1]]
        for group in groups:
            pieces = [stream[k * PIECES + i] for i in group]
            scale, *block, _ = lax.optimization_barrier((weight, *pieces, far[0]))
            at = slice(k * PIECES + group[0], k * PIECES + group[-1] + 1)
            staged = stage(staged, line[at], block, scale[None], mean[None], nc * local_frames)
        if k == nc - 2:
            early = staged[0]
    rows, level = staged
    level = level.sum(axis=1)
    count = nc * local_frames // npix
    if npix == 2:
        level = level[:count] + lax.ppermute(level[count:], "pix", [(0, 1), (1, 0)])
    else:
        level = lax.psum_scatter(level, "pix", scatter_dimension=0, tiled=True)
    row_scale = band_pixels / level
    extra = split(1.0 / mean)
    order = line[nc * PIECES : nc * PIECES + nc]
    order = jnp.stack([order, order])
    everything = nc * local_frames
    tile = 256 if count % 256 == 0 else local_frames
    tiles = lambda start, n: jnp.array([range(start, start + n), range(n)], jnp.int32)

    def correlate(name, cols, gate, ahead):
        other_core = [(0, 1), (1, 0)]
        if npix == 2 and ahead:
            slots = order[:, : nc - 1]
            sums, part = gram(early, local_frames, slots, nc, cols, extra, step=256)
            slots = order[:, nc - 1 :]
            (part,) = gram(rows, local_frames, slots, nc, cols, prev=part)
            total, theirs = part[:count], lax.ppermute(part[count:], "pix", other_core)
        elif npix == 2 and name == 2:
            n = count // tile
            sums, theirs = gram(rows, tile, tiles(n, n), n, cols, extra)
            theirs = lax.ppermute(theirs, "pix", other_core)
            (total,) = gram(rows, tile, tiles(0, n), n, cols)
        elif npix == 2:
            sums, theirs, total = gram_halves(rows, cols, extra)
            theirs = lax.ppermute(theirs, "pix", other_core)
        else:
            n = everything // tile
            sums, part = gram(rows, tile, tiles(0, n), n, cols, extra)
            total = lax.psum_scatter(part, "pix", scatter_dimension=0, tiled=True)
            theirs = jnp.zeros_like(total)
        sums = sums[:3].sum(axis=0)
        if npix == 2:
            sums = sums + lax.ppermute(sums, "pix", other_core)
        else:
            sums = lax.psum(sums, "pix")
        theirs, gate = lax.optimization_barrier((theirs, gate))
        return (total + theirs) * row_scale[:, None] * (1.0 / sums)[None, :]

    over = [(i, i ^ 2) for i in range(nc)]
    chunks = [[(k, 0, PIECES)] for k in range(nc - 1)] + [[(nc - 1, i, 1) for i in range(PIECES)]]
    gate, outs, n = row_scale, None, 0
    for parts in chunks:
        values, ships = [], []
        for k, i, size in parts:
            lo = k * PIECES + i
            value = correlate(n, near[lo : lo + size] + far[lo : lo + size], gate, k < 2)
            a, b = value[:, : size * height], value[:, size * height :]
            gate = (jnp.where(same, b, a) - 1.0).astype(SHIP)
            values.append(value)
            ships.append(lax.ppermute(gate, "tcol", over).astype(jnp.float32) + 1.0)
            n += 1
        at = nc * PIECES + nc + 2 * k
        info = jnp.concatenate([line[at : at + 2], flags])
        outs = place(outs, info, values, ships, nc * local_frames)
    return outs[0], outs[1]


def solution(mesh):
    in_specs = (P(("trow", "tcol"), None, "pix", None), P(("trow", "tcol"), None))
    out_specs = (P(("trow", "pix"), "tcol"), P(("trow", "pix"), "tcol"))

    return jax.shard_map(
        per_device, mesh=mesh, in_specs=in_specs, out_specs=out_specs, check_vma=False
    )
```
